32 devices in a mesh: dp: 4 (over y, x), fsdp: 8 (over z, core).
Axes of the slice: x: 2, y: 2, z: 4, core: 2. Of those that a mesh axis runs over, the one named last changes fastest.
Arguments:
- segment_input: bfloat16 [128, 32, 32, 512], P(('dp', 'fsdp')), may hold values from -256 to 256
- cotangent: bfloat16 [128, 16, 16, 1024], P(('dp', 'fsdp')), may hold values from -6 to 6
- tile_centres: int32 [128, 2], P(('dp', 'fsdp')), may hold values from 4 to 28
- valid_mask: int32 [128, 16, 16], P(('dp', 'fsdp')), may hold values from 0 to 1, as said below
- w_down: bfloat16 [512, 9, 1024], P('fsdp'), may hold values from -0.09375 to 0.09375
- w_split: bfloat16 [1024, 1, 1024], P('fsdp'), may hold values from -0.1875 to 0.1875
- w_reduce: bfloat16 [2, 512, 1, 512], P(None, 'fsdp'), may hold values from -0.25 to 0.25
- w_spread: bfloat16 [2, 512, 9, 512], P(None, 'fsdp'), may hold values from -0.09375 to 0.09375
- w_trans: bfloat16 [512, 1, 512], P('fsdp'), may hold values from -0.25 to 0.25
- w_unite: bfloat16 [1024, 1, 1024], P('fsdp'), may hold values from -0.1875 to 0.1875
- bn_gain: float32 [5632], replicated, may hold values from 0.1 to 1.9
- bn_bias: float32 [5632], replicated, may hold values from -3 to 3
- running_mean: float32 [5632], replicated, may hold values from -3 to 3
- running_var: float32 [5632], replicated, may hold values from 0.5 to 2
Outputs:
- output: bfloat16 [128, 16, 16, 1024], P(('dp', 'fsdp'))
- input_grad: bfloat16 [128, 32, 32, 512], P(('dp', 'fsdp'))
- grad_down: float32 [512, 9, 1024], P('fsdp')
- grad_split: float32 [1024, 1, 1024], P('fsdp')
- grad_reduce: float32 [2, 512, 1, 512], P(None, 'fsdp')
- grad_spread: float32 [2, 512, 9, 512], P(None, 'fsdp')
- grad_trans: float32 [512, 1, 512], P('fsdp')
- grad_unite: float32 [1024, 1, 1024], P('fsdp')
- grad_gain: float32 [5632], replicated
- grad_bias: float32 [5632], replicated
- new_running_mean: float32 [5632], replicated
- new_running_var: float32 [5632], replicated
The draws below stay inside these ranges and needn't reach their ends.
Inputs may be any that keep to these rules, and one draw needn't show every extreme that they name: `valid_mask`: 1 marks a pixel that enters the norms' statistics.
All inputs are finite; a program needn't handle non-finite values.
Results may differ from the reference program's by a relative error of at most 0.03.
Values may be sent and summed in bfloat16 or wider, within the bound.
No kernel may reach another device: no remote copies, remote signals or barrier semaphores. Data moves between devices by JAX's collectives and lax.ppermute only.
A program may use at most 384 MiB of HBM per device.

```python
import math
import jax
import jax.numpy as jnp
from jax import lax

WIDTH = 1024
HALF = 512
C_PREV = 512
SIDE = 16
BLOCKS = 2
IMAGES = 128
IN_SIDE = 32
NORM_CH = 5632


def letterbox(key):
    bands = jax.random.randint(jax.random.fold_in(key, 7), (IMAGES, 4), 0, SIDE // 4 + 1)
    coords = jnp.arange(SIDE, dtype=jnp.int32)
    rows_kept = (coords[None, :] >= bands[:, 0:1]) & (coords[None, :] < SIDE - bands[:, 1:2])
    cols_kept = (coords[None, :] >= bands[:, 2:3]) & (coords[None, :] < SIDE - bands[:, 3:4])
    return (rows_kept[:, :, None] & cols_kept[:, None, :]).astype(jnp.int32)


def draw_valid_mask(key, part):
    return letterbox(key)


def draw_segment_input(key, part):
    valid_fine = jnp.repeat(jnp.repeat(letterbox(key), 2, axis=1), 2, axis=2).astype(jnp.float32)[..., None]
    key_list = jax.random.split(jax.random.fold_in(key, 11), 4)
    images = jnp.arange(IMAGES, dtype=jnp.float32)
    jitter = jax.random.uniform(key_list[0], (IMAGES,), jnp.float32)
    channel_scale = jnp.exp(jax.random.uniform(key_list[1], (C_PREV,), jnp.float32, -1.15, 1.15))
    channel_mean = 0.5 * jax.random.normal(key_list[2], (C_PREV,), jnp.float32)
    full_shape = (IMAGES, IN_SIDE, IN_SIDE, C_PREV)
    image_scale = 10.0 ** ((images + jitter) / IMAGES)
    noise_draw = jnp.clip(jax.random.normal(key_list[3], full_shape, jnp.float32), -6.0, 6.0)
    features = (noise_draw * channel_scale + channel_mean) * image_scale[:, None, None, None]
    fill_value = 3.0 * image_scale[:, None, None, None]
    return (valid_fine * features + (1.0 - valid_fine) * fill_value).astype(jnp.bfloat16)


def plant(values, key, smallest, high):
    shape = values.shape
    index_at = [jax.random.randint(jax.random.fold_in(key, axis), (), 0, shape[axis]) for axis in range(len(shape))]
    values = values.at[tuple(index_at)].set(smallest)
    longest = shape.index(max(shape))
    index_at[longest] = (index_at[longest] + 1) % shape[longest]
    return values.at[tuple(index_at)].set(high)


def level_of(rng, dims, pieces, smallest, top_value):
    def one(position, shards_of):
        draws = jax.random.uniform(jax.random.fold_in(jax.random.fold_in(rng, 6), position), (shards_of,), jnp.float32, smallest / len(pieces), top_value / len(pieces))
        return jnp.repeat(jnp.exp(draws), dims[position] // shards_of).reshape((-1,) + (1,) * (len(dims) - position - 1))

    loudness = one(*pieces[0])
    for cut in pieces[1:]:
        loudness = loudness * one(*cut)
    return loudness


def bell_draw(own_key, shape, scale, most, cuts=(), held_as=jnp.bfloat16):
    loudness = level_of(own_key, shape, cuts, -0.22, 0.18) if cuts else 1.0
    values = jax.random.normal(own_key, shape, jnp.float32) * scale * loudness
    return jnp.minimum(jnp.maximum(values, -most), most).astype(held_as)


def setup_inputs(seed: int = 0) -> dict:
    streams_of = jax.random.split(jax.random.key(seed), 15)
    segment_input = draw_segment_input(jax.random.fold_in(streams_of[14], 71), 0)
    cotangent = bell_draw(streams_of[1], (IMAGES, SIDE, SIDE, WIDTH), 1.0, 6.0, ((0, 32),))
    tile_centres = plant(jax.random.randint(streams_of[2], (IMAGES, 2), IN_SIDE // 8, IN_SIDE - IN_SIDE // 8 + 1), jax.random.fold_in(streams_of[2], 1), IN_SIDE // 8, (IN_SIDE - IN_SIDE // 8 + 1) - 1).astype(jnp.int32)
    valid_mask = draw_valid_mask(jax.random.fold_in(streams_of[14], 71), 0)
    w_down = bell_draw(streams_of[4], (C_PREV, 9, WIDTH), (9 * C_PREV) ** -0.5, 0.09375, ((0, 8),))
    w_split = bell_draw(streams_of[5], (WIDTH, 1, 2 * HALF), WIDTH ** -0.5, 0.1875, ((0, 8),))
    w_reduce = bell_draw(streams_of[6], (BLOCKS, HALF, 1, HALF), HALF ** -0.5, 0.25, ((1, 8),))
    w_spread = bell_draw(streams_of[7], (BLOCKS, HALF, 9, HALF), (9 * HALF) ** -0.5, 0.09375, ((1, 8),))
    w_trans = bell_draw(streams_of[8], (HALF, 1, HALF), HALF ** -0.5, 0.25, ((0, 8),))
    w_unite = bell_draw(streams_of[9], (2 * HALF, 1, WIDTH), (2 * HALF) ** -0.5, 0.1875, ((0, 8),))
    bn_gain = jnp.clip(1.0 + 0.18 * jax.random.normal(streams_of[10], (NORM_CH,), jnp.float32), 0.1, 1.9)
    bn_bias = bell_draw(streams_of[11], (NORM_CH,), 0.5, 3.0, (), jnp.float32)
    running_mean = bell_draw(streams_of[12], (NORM_CH,), 0.5, 3.0, (), jnp.float32)
    running_var = jnp.clip(jnp.exp(jax.random.uniform(streams_of[13], (NORM_CH,), jnp.float32, math.log(0.5), math.log(2.0))), 0.5, 2.0)
    return {"segment_input": segment_input, "cotangent": cotangent, "tile_centres": tile_centres, "valid_mask": valid_mask, "w_down": w_down, "w_split": w_split, "w_reduce": w_reduce, "w_spread": w_spread, "w_trans": w_trans, "w_unite": w_unite, "bn_gain": bn_gain, "bn_bias": bn_bias, "running_mean": running_mean, "running_var": running_var}


@jax.custom_vjp
def low(v):
    return lax.optimization_barrier(v.astype(jnp.bfloat16)).astype(jnp.float32)

@jax.custom_vjp
def low_back(v):
    return v

def low_keep(v):
    return (low(v), None)

def low_pass(kept, grad):
    return (grad,)

def back_keep(v):
    return (v, None)

def back_low(kept, grad):
    return (low(grad),)
low.defvjp(low_keep, low_pass)
low_back.defvjp(back_keep, back_low)
norm_eps = 1e-05
momentum_rate = 0.1
exact_mode = lax.Precision.HIGHEST
group_images = 8

def mish_curve(values):
    return values * jnp.tanh(jax.nn.softplus(values))

def tile_masks(centres):
    extent = 2 * SIDE
    coords = jnp.arange(extent, dtype=jnp.int32)
    lower_half = (coords[None, :] >= centres[:, 0:1]).astype(jnp.int32)
    right_half = (coords[None, :] >= centres[:, 1:2]).astype(jnp.int32)
    tiles = 2 * lower_half[:, :, None] + right_half[:, None, :]
    fine_pad = jnp.pad(tiles, ((0, 0), (1, 1), (1, 1)), constant_values=-1)
    own_tile = tiles[:, ::2, ::2]
    coarse_pad = jnp.pad(own_tile, ((0, 0), (1, 1), (1, 1)), constant_values=-1)
    down_list = []
    mid_list = []
    for tap_index in range(9):
        row_step = tap_index // 3
        col_step = tap_index % 3
        down_list.append(fine_pad[:, row_step:row_step + extent:2, col_step:col_step + extent:2] == own_tile)
        mid_list.append(coarse_pad[:, row_step:row_step + SIDE, col_step:col_step + SIDE] == own_tile)
    return (jnp.stack(down_list, axis=-1).astype(jnp.float32), jnp.stack(mid_list, axis=-1).astype(jnp.float32))

def gather_taps(image_values, tap_masks, stride):
    extent = stride * SIDE
    padded = jnp.pad(image_values, ((0, 0), (1, 1), (1, 1), (0, 0)))
    tap_list = []
    for tap_index in range(9):
        row_step = tap_index // 3
        col_step = tap_index % 3
        window = padded[:, row_step:row_step + extent:stride, col_step:col_step + extent:stride, :]
        tap_list.append(window * tap_masks[..., tap_index:tap_index + 1])
    return jnp.stack(tap_list, axis=3)

def conv_three(image_values, tap_masks, weight, stride):
    groups = image_values.shape[0] // group_images
    shaped = image_values.reshape((groups, group_images) + image_values.shape[1:])
    masked = tap_masks.reshape((groups, group_images) + tap_masks.shape[1:])

    def one_group(group_pair):
        patches = gather_taps(group_pair[0], group_pair[1], stride)
        return jnp.einsum('nhwtc,cto->nhwo', patches, weight, precision=exact_mode)
    result = lax.map(jax.checkpoint(one_group), (shaped, masked))
    return result.reshape((image_values.shape[0], SIDE, SIDE, weight.shape[2]))

def conv_one(image_values, weight):
    return jnp.einsum('nhwc,co->nhwo', image_values, weight[:, 0, :], precision=exact_mode)

def norm_mish(conv_out, valid_float, valid_count, gain_slice, bias_slice):
    weights = valid_float[..., None]
    average = lax.optimization_barrier(jnp.sum(conv_out * weights, axis=(0, 1, 2))) / valid_count
    centred = conv_out - average
    variance = lax.optimization_barrier(jnp.sum(weights * centred * centred, axis=(0, 1, 2))) / valid_count
    normed = centred * lax.rsqrt(variance + norm_eps)
    return (mish_curve(gain_slice * normed + bias_slice), average, variance)

def reference(segment_input, cotangent, tile_centres, valid_mask, w_down, w_split, w_reduce, w_spread, w_trans, w_unite, bn_gain, bn_bias, running_mean, running_var):
    same_down, same_mid = tile_masks(tile_centres)
    valid_float = valid_mask.astype(jnp.float32)
    valid_count = jnp.sum(valid_float)

    def forward(image_values, down_weight, split_weight, reduce_weights, spread_weights, trans_weight, unite_weight, gain_vector, bias_vector):
        moments = []

        def norm_layer(conv_out):
            offset = sum((moment[0].shape[0] for moment in moments))
            channels = conv_out.shape[-1]
            activity, average, variance = norm_mish(low_back(conv_out), valid_float, valid_count, gain_vector[offset:offset + channels], bias_vector[offset:offset + channels])
            moments.append((average, variance))
            return activity
        down_act = norm_layer(conv_three(image_values, same_down, down_weight, 2))
        split_act = norm_layer(conv_one(low(down_act), split_weight))
        route_act = split_act[..., :HALF]
        residual_stream = split_act[..., HALF:]
        for block_index in range(BLOCKS):
            inner_act = norm_layer(conv_one(low(residual_stream), reduce_weights[block_index]))
            residual_stream = residual_stream + norm_layer(conv_three(low(inner_act), same_mid, spread_weights[block_index], 1))
        trans_act = norm_layer(conv_one(low(residual_stream), trans_weight))
        joined = low(jnp.concatenate([route_act, trans_act], axis=-1))
        result = norm_layer(conv_one(joined, unite_weight))
        means = jnp.concatenate([moment[0] for moment in moments])
        variances = jnp.concatenate([moment[1] for moment in moments])
        return (result, (means, variances))
    primals = (segment_input.astype(jnp.float32), w_down.astype(jnp.float32), w_split.astype(jnp.float32), w_reduce.astype(jnp.float32), w_spread.astype(jnp.float32), w_trans.astype(jnp.float32), w_unite.astype(jnp.float32), bn_gain, bn_bias)
    result, pullback, stats = jax.vjp(forward, *primals, has_aux=True)
    grads = pullback(cotangent.astype(jnp.float32))
    new_mean = (1.0 - momentum_rate) * running_mean + momentum_rate * stats[0]
    new_var = (1.0 - momentum_rate) * running_var + momentum_rate * stats[1] * valid_count / (valid_count - 1.0)
    return (result.astype(jnp.bfloat16), grads[0].astype(jnp.bfloat16), grads[1], grads[2], grads[3], grads[4], grads[5], grads[6], grads[7], grads[8], new_mean, new_var)
```

```python
import functools

import jax
import jax.numpy as jnp
from jax import lax
from jax.experimental import pallas as pl
from jax.experimental.pallas import tpu as pltpu
from jax.sharding import PartitionSpec as P

norm_eps = 1e-05
momentum_rate = 0.1
ALL = ("dp", "fsdp")
F32 = jnp.float32
BF16 = jnp.bfloat16
VMEM_LIMIT = 58 * 1024 * 1024


def params():
    return pltpu.CompilerParams(vmem_limit_bytes=VMEM_LIMIT)


def tile_masks(centres, grid_side):
    extent = 2 * grid_side
    coords = jnp.arange(extent, dtype=jnp.int32)
    lower_half = (coords[None, :] >= centres[:, 0:1]).astype(jnp.int32)
    right_half = (coords[None, :] >= centres[:, 1:2]).astype(jnp.int32)
    tiles = 2 * lower_half[:, :, None] + right_half[:, None, :]
    fine_pad = jnp.pad(tiles, ((0, 0), (1, 1), (1, 1)), constant_values=-1)
    own_tile = tiles[:, ::2, ::2]
    coarse_pad = jnp.pad(own_tile, ((0, 0), (1, 1), (1, 1)), constant_values=-1)
    down_list, back_list, mid_list = [], [], []
    for a in range(3):
        for b in range(3):
            down = (
                fine_pad[:, a : a + extent : 2, b : b + extent : 2] == own_tile
            ).astype(F32)
            down_list.append(down)
            rows, cols = int(a == 0), int(b == 0)
            back_list.append(jnp.pad(down, ((0, 0), (0, rows), (0, cols)))[:, rows:, cols:])
            mid_list.append(
                (coarse_pad[:, a : a + grid_side, b : b + grid_side] == own_tile).astype(F32)
            )

    def lanes(parts):
        flat = jnp.stack(parts).reshape(9, -1, 1)
        return jnp.broadcast_to(flat, (9, flat.shape[1], 128)).astype(BF16)

    return lanes(down_list), lanes(back_list), lanes(mid_list)


def mish_parts(y):
    u = jnp.exp(-jnp.abs(y))
    pos = y > 0.0
    num = jnp.where(pos, 1.0 + 2.0 * u, u * (u + 2.0))
    gap = jnp.where(pos, 2.0 * u * u, 2.0)
    return u, pos, num, gap, num + gap


def mish(y):
    _, _, num, _, den = mish_parts(y)
    return y * (num / den)


def mish_slope(y):
    u, pos, num, gap, den = mish_parts(y)
    once = 1.0 + u
    both = 1.0 / (den * once)
    inv = both * once
    sig = jnp.where(pos, 1.0, u) * (both * den)
    return num * inv + y * sig * (gap * inv) * ((den + num) * inv)


def mish_both(y):
    u, pos, num, gap, den = mish_parts(y)
    once = 1.0 + u
    both = 1.0 / (den * once)
    inv = both * once
    sig = jnp.where(pos, 1.0, u) * (both * den)
    tan = num * inv
    return y * tan, tan + y * sig * (gap * inv) * ((den + num) * inv)


def col_shift(x, step):
    if step == 0:
        return x
    rows = x.shape[0]
    return pltpu.roll(x.astype(F32), (-step) % rows, 0).astype(BF16)


def row_shift(x, step):
    if step == 0:
        return x
    if step > 0:
        return jnp.concatenate([x[step:], x[:step]], axis=0)
    return jnp.concatenate([x[step:], x[: x.shape[0] + step]], axis=0)


def masked(x, lane_mask):
    reps = x.shape[1] // 128
    return x * jnp.concatenate([lane_mask] * reps, axis=1)


def tap_weight(w_ref, tap):
    w = w_ref[:, tap]
    return w.reshape(w.shape[0] * w.shape[1], w.shape[2])


def dot_nn(a, b):
    return lax.dot_general(a, b, (((1,), (0,)), ((), ())), preferred_element_type=F32)


def dot_nt(a, b):
    return lax.dot_general(a, b, (((1,), (1,)), ((), ())), preferred_element_type=F32)


def dot_tn(a, b):
    return lax.dot_general(a, b, (((0,), (0,)), ((), ())), preferred_element_type=F32)


def mid_taps(x, side):
    cols = [col_shift(x, b - 1) for b in range(3)]
    for tap in range(9):
        a, b = divmod(tap, 3)
        yield tap, row_shift(cols[b], side * (a - 1))


def down_taps(phase, side):
    cols = {}
    for pr in range(2):
        for b in range(3):
            x = phase(2 * pr + int(b != 1))
            cols[pr, b] = col_shift(x, -1) if b == 0 else x
    for tap in range(9):
        a, b = divmod(tap, 3)
        yield tap, row_shift(cols[int(a != 1), b], -side if a == 0 else 0)


def device_total(s_ref):
    count, _, channels = s_ref.shape
    start = jnp.zeros((2, channels), F32)
    return lax.fori_loop(0, count, lambda i, t: t + s_ref[i], start, unroll=8)


def moments(s_ref, cnt_ref):
    count = s_ref.shape[0]
    total = device_total(s_ref)
    inv_n = cnt_ref[2 * count + 1]
    mean = total[0:1] * inv_n

    def spread(i, t):
        d = s_ref[i][0:1] - cnt_ref[i] * mean
        return t + d * d * cnt_ref[count + i]

    between = lax.fori_loop(0, count, spread, jnp.zeros_like(mean), unroll=8)
    var = (total[1:2] + between) * inv_n
    return mean, var, lax.rsqrt(var + norm_eps)


def write_moments(mv_ref, mean, var, inv):
    mv_ref[0:1] = mean
    mv_ref[1:2] = var
    mv_ref[2:3] = inv
    mv_ref[3:8] = jnp.zeros((5, mean.shape[1]), F32)


def collect_moments(out, valid, acc_ref, num_ref, st_ref):
    step = pl.program_id(0)
    n = jnp.sum(valid, axis=0, keepdims=True)
    total = jnp.sum(out * valid, axis=0, keepdims=True)
    mean = total / jnp.maximum(n, 1.0)
    centred = out - mean
    squares = jnp.sum(valid * centred * centred, axis=0, keepdims=True)

    @pl.when(step == 0)
    def _():
        acc_ref[0:1] = total
        acc_ref[1:2] = squares
        num_ref[0:1] = jnp.broadcast_to(n, (1, 128))

    @pl.when(step > 0)
    def _():
        n_old = num_ref[0:1, 0:1]
        n_new = n_old + n
        old_mean = acc_ref[0:1] / jnp.maximum(n_old, 1.0)
        gap = mean - old_mean
        acc_ref[0:1] = acc_ref[0:1] + total
        acc_ref[1:2] = acc_ref[1:2] + squares + gap * gap * (n * n_old / jnp.maximum(n_new, 1.0))
        num_ref[0:1] = jnp.broadcast_to(n_new, (1, 128))

    @pl.when(step == pl.num_programs(0) - 1)
    def _():
        st_ref[...] = jnp.broadcast_to(acc_ref[0:2][None], st_ref.shape)


def collect_sums(g, xhat, acc_ref, st_ref):
    step = pl.program_id(0)
    first = jnp.sum(g, axis=0, keepdims=True)
    second = jnp.sum(g * xhat, axis=0, keepdims=True)

    @pl.when(step == 0)
    def _():
        acc_ref[0:1] = first
        acc_ref[1:2] = second

    @pl.when(step > 0)
    def _():
        acc_ref[0:1] = acc_ref[0:1] + first
        acc_ref[1:2] = acc_ref[1:2] + second

    @pl.when(step == pl.num_programs(0) - 1)
    def _():
        st_ref[...] = jnp.broadcast_to(acc_ref[0:2][None], st_ref.shape)


def prep_kernel(x_ref, ph_ref):
    half = ph_ref.shape[1]
    p = lax.broadcasted_iota(jnp.int32, (half, 2 * half), 0)
    s = lax.broadcasted_iota(jnp.int32, (half, 2 * half), 1)
    for pr in range(2):
        x = x_ref[0, :, pr]
        x = x.reshape(2 * half, x.shape[-1])
        for pc in range(2):
            pick = jnp.where(s == 2 * p + pc, 1.0, 0.0).astype(BF16)
            ph_ref[2 * pr + pc] = dot_nn(pick, x).astype(BF16)


def first_kernel(side, ph_ref, m_ref, valid_ref, w_ref, z_ref, st_ref, acc_ref, num_ref):
    out = None
    for tap, x in down_taps(lambda k: ph_ref[k], side):
        part = dot_nn(masked(x, m_ref[tap]), tap_weight(w_ref, tap))
        out = part if out is None else out + part
    z_ref[...] = out
    collect_moments(out, valid_ref[...], acc_ref, num_ref, st_ref)


def forward_kernel(kind, side, z_ref, s_ref, cnt_ref, gain_ref, bias_ref, valid_ref, w_ref, *rest):
    rest = list(rest)
    m_ref = rest.pop(0) if kind == "three" else None
    other_ref = rest.pop(0) if kind in ("resid", "join") else None
    v_ref = rest.pop(0)
    keep_ref = rest.pop(0) if kind in ("split", "resid") else None
    mv_ref, out_ref, st_ref, acc_ref, num_ref = rest
    mean, var, inv = moments(s_ref, cnt_ref)

    @pl.when(pl.program_id(0) == 0)
    def _():
        write_moments(mv_ref, mean, var, inv)

    act = mish(((z_ref[...] - mean) * inv) * gain_ref[...] + bias_ref[...])
    if kind == "split":
        half = act.shape[1] // 2
        low = act.astype(BF16)
        v_ref[...] = low
        keep_ref[...] = act[:, half:]
        v = low[:, half:]
    elif kind == "resid":
        act = other_ref[...] + act
        keep_ref[...] = act
        v = act.astype(BF16)
        v_ref[...] = v
    elif kind == "join":
        v = jnp.concatenate([other_ref[...], act.astype(BF16)], axis=1)
        v_ref[...] = v
    else:
        v = act.astype(BF16)
        v_ref[...] = v
    if kind == "three":
        out = None
        for tap, x in mid_taps(v, side):
            part = dot_nn(masked(x, m_ref[tap]), tap_weight(w_ref, tap))
            out = part if out is None else out + part
    else:
        out = dot_nn(v, w_ref[...])
    out_ref[...] = out
    collect_moments(out, valid_ref[...], acc_ref, num_ref, st_ref)


def top_kernel(
    z_ref, s_ref, cnt_ref, gain_ref, bias_ref, cot_ref, o_ref, mv_ref, g_ref, st_ref, acc_ref
):
    mean, var, inv = moments(s_ref, cnt_ref)

    @pl.when(pl.program_id(0) == 0)
    def _():
        write_moments(mv_ref, mean, var, inv)

    xhat = (z_ref[...] - mean) * inv
    act, slope = mish_both(xhat * gain_ref[...] + bias_ref[...])
    o_ref[...] = act.astype(BF16)
    g = cot_ref[...].astype(F32) * slope
    g_ref[...] = g
    collect_sums(g, xhat, acc_ref, st_ref)


def norm_grad(g_ref, z_ref, mv_ref, s_ref, gain_ref, valid_ref, cnt_ref, tot_ref):
    total = device_total(s_ref)

    @pl.when(pl.program_id(0) == 0)
    def _():
        tot_ref[0:2] = total
        tot_ref[2:8] = jnp.zeros((6, total.shape[1]), F32)

    inv = mv_ref[2:3]
    inv_n = cnt_ref[2 * s_ref.shape[0] + 1]
    xhat = (z_ref[...] - mv_ref[0:1]) * inv
    mean_part = (valid_ref[...] * inv_n) * (total[0:1] + xhat * total[1:2])
    return (gain_ref[...] * inv * (g_ref[...] - mean_part)).astype(BF16)


def backward_kernel(
    kind,
    side,
    g_ref,
    z_ref,
    mv_ref,
    s_ref,
    gain_ref,
    valid_ref,
    cnt_ref,
    w_ref,
    zp_ref,
    mvp_ref,
    gainp_ref,
    biasp_ref,
    *rest,
):
    rest = list(rest)
    m_ref = rest.pop(0) if kind == "three" else None
    add_ref = rest.pop(0) if kind in ("add", "merge") else None
    route_ref = rest.pop(0) if kind == "merge" else None
    dz_ref, tot_ref = rest.pop(0), rest.pop(0)
    keep_ref = rest.pop(0) if kind in ("part", "keep", "add") else None
    gp_ref, st_ref, acc_ref = rest
    dz = norm_grad(g_ref, z_ref, mv_ref, s_ref, gain_ref, valid_ref, cnt_ref, tot_ref)
    dz_ref[...] = dz
    if kind == "three":
        ga = None
        for tap, x in mid_taps(dz, side):
            part = dot_nt(masked(x, m_ref[tap]), tap_weight(w_ref, 8 - tap))
            ga = part if ga is None else ga + part
    else:
        ga = dot_nt(dz, w_ref[...])
    if kind == "part":
        half = ga.shape[1] // 2
        keep_ref[...] = ga[:, :half]
        ga = ga[:, half:]
    elif kind == "keep":
        keep_ref[...] = ga
    elif kind == "add":
        ga = ga + add_ref[...]
        keep_ref[...] = ga
    elif kind == "merge":
        ga = jnp.concatenate([route_ref[...], ga + add_ref[...]], axis=1)
    xhat = (zp_ref[...] - mvp_ref[0:1]) * mvp_ref[2:3]
    gp = ga * mish_slope(xhat * gainp_ref[...] + biasp_ref[...])
    gp_ref[...] = gp
    collect_sums(gp, xhat, acc_ref, st_ref)


def last_norm_kernel(
    g_ref, z_ref, mv_ref, s_ref, gain_ref, valid_ref, cnt_ref, dz_ref, tot_ref
):
    dz_ref[...] = norm_grad(g_ref, z_ref, mv_ref, s_ref, gain_ref, valid_ref, cnt_ref, tot_ref)


def input_grad_kernel(side, dz_ref, m_ref, w_ref, o_ref):
    dz = dz_ref[...]
    rows = dz.shape[0]
    moved = {}
    for dj in range(2):
        base = col_shift(dz, dj)
        for di in range(2):
            moved[di, dj] = row_shift(base, side * di)
    s = lax.broadcasted_iota(jnp.int32, (2 * rows, 2 * rows), 0)
    k = lax.broadcasted_iota(jnp.int32, (2 * rows, 2 * rows), 1)
    source = jnp.where(k < rows, 2 * k, 2 * (k - rows) + 1)
    put = jnp.where(s == source, 1.0, 0.0).astype(BF16)
    choices = (((1, 0),), ((2, 0), (0, 1)))
    for pr in range(2):
        both = []
        for pc in range(2):
            total = None
            for a, di in choices[pr]:
                for b, dj in choices[pc]:
                    tap = 3 * a + b
                    part = dot_nt(masked(moved[di, dj], m_ref[tap]), tap_weight(w_ref, tap))
                    total = part if total is None else total + part
            both.append(total.astype(BF16))
        out = dot_nn(put, jnp.concatenate(both, axis=0)).astype(BF16)
        o_ref[0, :, pr] = out.reshape(side, 2 * side, out.shape[1])


def weight_grad_kernel(stride, side, x_ref, m_ref, dz_ref, o_ref):
    dz = dz_ref[...]
    taps = mid_taps(x_ref[...], side) if stride == 1 else down_taps(lambda k: x_ref[k], side)
    for tap, x in taps:
        grad = dot_tn(masked(x, m_ref[tap]), dz).astype(BF16)
        o_ref[:, tap] = grad.reshape(o_ref.shape[0], o_ref.shape[2], o_ref.shape[3])


def per_device(
    segment_input,
    cotangent,
    tile_centres,
    valid_mask,
    w_down,
    w_split,
    w_reduce,
    w_spread,
    w_trans,
    w_unite,
    bn_gain,
    bn_bias,
    running_mean,
    running_var,
):
    images, side, _, width = cotangent.shape
    half = w_trans.shape[2]
    c_prev = segment_input.shape[3]
    blocks = w_reduce.shape[0]
    per_image = side * side
    pixels = images * per_image
    fsdp = lax.axis_size("fsdp")
    devices = lax.axis_size("dp") * fsdp
    steps = images
    rows = pixels // steps

    def gather(shard):
        return lax.all_gather(shard, "fsdp", axis=0, tiled=False)

    full_down = gather(w_down.transpose(1, 0, 2))
    full_split = lax.all_gather(w_split[:, 0], "fsdp", axis=0, tiled=True)
    full_unite = lax.all_gather(w_unite[:, 0], "fsdp", axis=0, tiled=True)
    narrow = lax.all_gather(
        jnp.concatenate([w_reduce[b, :, 0] for b in range(blocks)] + [w_trans[:, 0]], axis=1),
        "fsdp",
        axis=0,
        tiled=True,
    )
    full_spread = [gather(w_spread[b].transpose(1, 0, 2)) for b in range(blocks)]

    mask_down, mask_back, mask_mid = tile_masks(tile_centres, side)
    valid = valid_mask.astype(F32).reshape(pixels, 1)
    own_count = jnp.broadcast_to(jnp.sum(valid), (devices, 1, 128))
    counts = lax.all_to_all(own_count, ALL, 0, 0, tiled=True)[:, 0, 0]
    whole_count = jnp.sum(counts)
    cnt = jnp.concatenate(
        [counts, 1.0 / jnp.maximum(counts, 1.0), jnp.stack([whole_count, 1.0 / whole_count])]
    )

    def exchange(st):
        return lax.all_to_all(st, ALL, 0, 0, tiled=True)

    smem = pl.BlockSpec(memory_space=pltpu.SMEM)

    def fixed(shape):
        return pl.BlockSpec(shape, lambda i: (0,) * len(shape))

    def single(shape, index=None):
        index = index or (0,) * len(shape)
        return pl.BlockSpec(shape, lambda i: index, pipeline_mode=pl.Buffered(1))

    def tall(channels, column=0):
        return pl.BlockSpec((rows, channels), lambda i: (i, column))

    mask_spec = pl.BlockSpec((9, rows, 128), lambda i: (0, i, 0))
    valid_spec = pl.BlockSpec((rows, 1), lambda i: (i, 0))

    def shaped(shape, dtype):
        return jax.ShapeDtypeStruct(shape, dtype)

    def stat_shape(channels):
        return shaped((devices, 2, channels), F32)

    widths = [width, width] + [half] * (2 * blocks) + [half, width]
    starts = [sum(widths[:i]) for i in range(len(widths))]
    gains = [bn_gain[s : s + c].reshape(1, c) for s, c in zip(starts, widths)]
    biases = [bn_bias[s : s + c].reshape(1, c) for s, c in zip(starts, widths)]
    layers = len(widths)

    weights = [None] * layers
    weights[0] = (full_down, single(full_down.shape))
    weights[1] = (full_split, single(full_split.shape))
    for b in range(blocks):
        weights[2 + 2 * b] = (narrow, single((half, half), (0, b)))
        weights[3 + 2 * b] = (full_spread[b], single(full_spread[b].shape))
    weights[layers - 2] = (narrow, single((half, half), (0, blocks)))
    weights[layers - 1] = (full_unite, single(full_unite.shape))

    x6 = segment_input.reshape(images, side, 2, 2 * side, c_prev)
    phases = pl.pallas_call(
        prep_kernel,
        grid=(images,),
        in_specs=[pl.BlockSpec((1, side, 2, 2 * side, c_prev), lambda i: (i, 0, 0, 0, 0))],
        out_specs=pl.BlockSpec((4, per_image, c_prev), lambda i: (0, i, 0)),
        out_shape=shaped((4, pixels, c_prev), BF16),
        compiler_params=params(),
        name="parity_images",
    )(x6)

    def scratch(channels):
        return [pltpu.VMEM((8, channels), F32), pltpu.VMEM((8, 128), F32)]

    z, st = [None] * layers, [None] * layers
    z[0], st[0] = pl.pallas_call(
        functools.partial(first_kernel, side),
        grid=(steps,),
        in_specs=[
            pl.BlockSpec((4, rows, c_prev), lambda i: (0, i, 0)),
            mask_spec,
            valid_spec,
            weights[0][1],
        ],
        out_specs=[tall(width), fixed((devices, 2, width))],
        out_shape=[shaped((pixels, width), F32), stat_shape(width)],
        scratch_shapes=scratch(width),
        compiler_params=params(),
        name="down_forward",
    )(phases, mask_down, valid, full_down)

    inputs = [None] * layers
    moment = [None] * layers

    def forward(layer, kind, extra=(), extra_specs=()):
        prev, channels = layer - 1, widths[layer - 1]
        w, w_spec = weights[layer]
        gathered = exchange(st[prev])
        args = [z[prev], gathered, cnt, gains[prev], biases[prev], valid, w, *extra]
        specs = [
            tall(channels),
            fixed((devices, 2, channels)),
            smem,
            fixed((1, channels)),
            fixed((1, channels)),
            valid_spec,
            w_spec,
            *extra_specs,
        ]
        v_width = 2 * half if kind == "join" else channels
        out_specs, out_shape = [tall(v_width)], [shaped((pixels, v_width), BF16)]
        if kind in ("split", "resid"):
            out_specs.append(tall(half))
            out_shape.append(shaped((pixels, half), F32))
        n = widths[layer]
        out_specs += [fixed((8, channels)), tall(n), fixed((devices, 2, n))]
        out_shape += [shaped((8, channels), F32), shaped((pixels, n), F32), stat_shape(n)]
        outs = list(
            pl.pallas_call(
                functools.partial(forward_kernel, kind, side),
                grid=(steps,),
                in_specs=specs,
                out_specs=out_specs,
                out_shape=out_shape,
                scratch_shapes=scratch(n),
                compiler_params=params(),
                name="forward_" + kind,
            )(*args)
        )
        inputs[layer] = outs.pop(0)
        keep = outs.pop(0) if kind in ("split", "resid") else None
        moment[prev], z[layer], st[layer] = outs
        return keep

    forward(1, "plain")
    stream = None
    for b in range(blocks):
        if b == 0:
            stream = forward(2, "split")
        else:
            stream = forward(2 + 2 * b, "resid", (stream,), (tall(half),))
        forward(3 + 2 * b, "three", (mask_mid,), (mask_spec,))
    forward(layers - 2, "resid", (stream,), (tall(half),))
    split_low = inputs[2]
    forward(layers - 1, "join", (split_low,), (tall(half),))

    last = layers - 1
    n = widths[last]
    output, moment[last], g, st_back = pl.pallas_call(
        top_kernel,
        grid=(steps,),
        in_specs=[
            tall(n),
            fixed((devices, 2, n)),
            smem,
            fixed((1, n)),
            fixed((1, n)),
            tall(n),
        ],
        out_specs=[tall(n), fixed((8, n)), tall(n), fixed((devices, 2, n))],
        out_shape=[
            shaped((pixels, n), BF16),
            shaped((8, n), F32),
            shaped((pixels, n), F32),
            stat_shape(n),
        ],
        scratch_shapes=[pltpu.VMEM((8, n), F32)],
        compiler_params=params(),
        name="top",
    )(z[last], exchange(st[last]), cnt, gains[last], biases[last], cotangent.reshape(pixels, n))

    totals = [None] * layers
    dz = [None] * layers

    def backward(layer, kind, g, gathered, extra=(), extra_specs=()):
        prev, channels = layer - 1, widths[layer]
        cp = widths[prev]
        w, w_spec = weights[layer]
        args = [g, z[layer], moment[layer], gathered, gains[layer], valid, cnt, w]
        args += [z[prev], moment[prev], gains[prev], biases[prev], *extra]
        specs = [
            tall(channels),
            tall(channels),
            fixed((8, channels)),
            fixed((devices, 2, channels)),
            fixed((1, channels)),
            valid_spec,
            smem,
            w_spec,
            tall(cp),
            fixed((8, cp)),
            fixed((1, cp)),
            fixed((1, cp)),
            *extra_specs,
        ]
        out_specs = [tall(channels), fixed((8, channels))]
        out_shape = [shaped((pixels, channels), BF16), shaped((8, channels), F32)]
        if kind in ("part", "keep", "add"):
            out_specs.append(tall(half))
            out_shape.append(shaped((pixels, half), F32))
        out_specs += [tall(cp), fixed((devices, 2, cp))]
        out_shape += [shaped((pixels, cp), F32), stat_shape(cp)]
        outs = list(
            pl.pallas_call(
                functools.partial(backward_kernel, kind, side),
                grid=(steps,),
                in_specs=specs,
                out_specs=out_specs,
                out_shape=out_shape,
                scratch_shapes=[pltpu.VMEM((8, cp), F32)],
                compiler_params=params(),
                name="backward_" + kind,
            )(*args)
        )
        dz[layer], totals[layer] = outs.pop(0), outs.pop(0)
        keep = outs.pop(0) if kind in ("part", "keep", "add") else None
        return outs[0], outs[1], keep

    def tap_grad(stride, x, lane_mask, dz_low, w_shape):
        return pl.pallas_call(
            functools.partial(weight_grad_kernel, stride, side),
            out_shape=shaped(w_shape, BF16),
            compiler_params=params(),
            name="weight_grad_" + str(stride),
        )(x, lane_mask, dz_low)

    def flat_grad(x, dz_low):
        return jnp.einsum("pk,pn->kn", x, dz_low, preferred_element_type=F32).astype(BF16)

    def scatter(grad):
        return lax.psum_scatter(grad, "fsdp", scatter_dimension=0, tiled=True)

    def sum_over_groups(own):
        groups = lax.axis_size("dp")
        parts = own.reshape(groups, own.shape[0] // groups, own.shape[1])
        parts = lax.all_to_all(parts, "dp", 0, 0, tiled=True)
        part = jnp.sum(parts.astype(F32), axis=0).astype(BF16)
        back = lax.all_to_all(
            jnp.broadcast_to(part[None], (groups, *part.shape)), "dp", 0, 0, tiled=True
        )
        return back.reshape(own.shape).astype(F32)

    def beside(st_back, grad, *due):
        return lax.optimization_barrier((exchange(st_back), grad, *due))[0]

    g, st_back, grad_route = backward(last, "part", g, exchange(st_back))
    grad_unite = flat_grad(inputs[last], dz[last])
    own_unite = scatter(grad_unite)
    g, st_back, grad_stream = backward(last - 1, "keep", g, beside(st_back, grad_unite))
    narrow_grads = [None] * (blocks + 1)
    narrow_grads[blocks] = flat_grad(inputs[last - 1], dz[last - 1])
    gathered = beside(st_back, narrow_grads[blocks])
    own_spread = [None] * blocks
    for b in reversed(range(blocks)):
        layer = 3 + 2 * b
        g, st_back, _ = backward(layer, "three", g, gathered, (mask_mid,), (mask_spec,))
        own = tap_grad(1, inputs[layer], mask_mid, dz[layer], full_spread[b].shape)
        due = (own_unite,) if b == blocks - 1 else ()
        gathered = beside(st_back, own, *due)
        own_spread[b] = scatter(own)
        layer = 2 + 2 * b
        if b > 0:
            g, st_back, grad_stream = backward(
                layer, "add", g, gathered, (grad_stream,), (tall(half),)
            )
            low = inputs[layer]
        else:
            g, st_back, _ = backward(
                layer, "merge", g, gathered, (grad_stream, grad_route), (tall(half), tall(half))
            )
            low = inputs[layer][:, half:]
        narrow_grads[b] = flat_grad(low, dz[layer])
        due = own_spread[1:2] if b == 0 else ()
        gathered = beside(st_back, narrow_grads[b], *due)
    own_narrow = scatter(jnp.concatenate(narrow_grads, axis=1))
    g, st_back, _ = backward(1, "plain", g, gathered)
    grad_split = flat_grad(inputs[1], dz[1])
    own_split = scatter(grad_split)
    dz[0], totals[0] = pl.pallas_call(
        last_norm_kernel,
        grid=(steps,),
        in_specs=[
            tall(width),
            tall(width),
            fixed((8, width)),
            fixed((devices, 2, width)),
            fixed((1, width)),
            valid_spec,
            smem,
        ],
        out_specs=[tall(width), fixed((8, width))],
        out_shape=[shaped((pixels, width), BF16), shaped((8, width), F32)],
        compiler_params=params(),
        name="down_norm",
    )(g, z[0], moment[0], beside(st_back, grad_split, own_spread[0]), gains[0], valid, cnt)
    grad_down = tap_grad(2, phases, mask_down, dz[0], full_down.shape)
    own_down = scatter(grad_down)
    dz_low, _ = lax.optimization_barrier((dz[0], grad_down))
    input_grad = pl.pallas_call(
        functools.partial(input_grad_kernel, side),
        grid=(images,),
        in_specs=[
            pl.BlockSpec((per_image, width), lambda i: (i, 0)),
            pl.BlockSpec((9, per_image, 128), lambda i: (0, i, 0)),
            weights[0][1],
        ],
        out_specs=pl.BlockSpec((1, side, 2, 2 * side, c_prev), lambda i: (i, 0, 0, 0, 0)),
        out_shape=shaped(x6.shape, BF16),
        compiler_params=params(),
        name="input_grad",
    )(dz_low, mask_back, full_down).reshape(segment_input.shape)

    packed = [own_unite, own_split, own_narrow, *own_spread]
    flat = [o.reshape(-1, half) for o in packed]
    sums = sum_over_groups(jnp.concatenate(flat, axis=0))
    ends = [0]
    for f in flat:
        ends.append(ends[-1] + f.shape[0])
    pieces = [sums[a:e].reshape(o.shape) for a, e, o in zip(ends, ends[1:], packed)]
    grad_unite, grad_split, narrow_grad = pieces[:3]
    spread_grads = [piece[0].transpose(1, 0, 2) for piece in pieces[3:]]
    grad_down = sum_over_groups(own_down.reshape(-1, width)).reshape(own_down.shape)
    grad_down = grad_down[0].transpose(1, 0, 2)

    means = jnp.concatenate([m[0] for m in moment])
    variances = jnp.concatenate([m[1] for m in moment])
    new_mean = (1.0 - momentum_rate) * running_mean + momentum_rate * means
    new_var = (1.0 - momentum_rate) * running_var + momentum_rate * variances * whole_count / (
        whole_count - 1.0
    )
    grad_reduce = jnp.stack([narrow_grad[:, None, half * b : half * (b + 1)] for b in range(blocks)])
    return (
        output.reshape(cotangent.shape),
        input_grad,
        grad_down,
        grad_split[:, None],
        grad_reduce,
        jnp.stack(spread_grads),
        narrow_grad[:, None, half * blocks :],
        grad_unite[:, None],
        jnp.concatenate([t[1] for t in totals]),
        jnp.concatenate([t[0] for t in totals]),
        new_mean,
        new_var,
    )


def solution(mesh):
    image = P(ALL, None, None, None)
    row3 = P("fsdp", None, None)
    row4 = P(None, "fsdp", None, None)
    return jax.shard_map(
        per_device,
        mesh=mesh,
        in_specs=(
            image,
            image,
            P(ALL, None),
            P(ALL, None, None),
            row3,
            row3,
            row4,
            row4,
            row3,
            row3,
            P(),
            P(),
            P(),
            P(),
        ),
        out_specs=(image, image, row3, row3, row4, row4, row3, row3, P(), P(), P(), P()),
        check_vma=False,
    )
```

```python
import functools

import jax
import jax.numpy as jnp
from jax import lax
from jax.experimental import pallas as pl
from jax.experimental.pallas import tpu as pltpu
from jax.sharding import PartitionSpec as P

norm_eps = 1e-05
momentum_rate = 0.1
ALL = ("dp", "fsdp")
F32 = jnp.float32
BF16 = jnp.bfloat16
VMEM_LIMIT = 58 * 1024 * 1024


def params():
    return pltpu.CompilerParams(vmem_limit_bytes=VMEM_LIMIT)


def cost(products, elements):
    return pl.CostEstimate(flops=2 * products, transcendentals=0, bytes_accessed=4 * elements)


def mish_parts(y):
    u = jnp.exp(-jnp.abs(y))
    pos = y > 0.0
    num = jnp.where(pos, 1.0 + 2.0 * u, u * (u + 2.0))
    gap = jnp.where(pos, 2.0 * u * u, 2.0)
    return u, pos, num, gap, num + gap


def mish(y):
    _, _, num, _, den = mish_parts(y)
    return y * (num / den)


def mish_slope(y):
    u, pos, num, gap, den = mish_parts(y)
    once = 1.0 + u
    both = 1.0 / (den * once)
    inv = both * once
    sig = jnp.where(pos, 1.0, u) * (both * den)
    return num * inv + y * sig * (gap * inv) * ((den + num) * inv)


def mish_both(y):
    u, pos, num, gap, den = mish_parts(y)
    once = 1.0 + u
    both = 1.0 / (den * once)
    inv = both * once
    sig = jnp.where(pos, 1.0, u) * (both * den)
    tan = num * inv
    return y * tan, tan + y * sig * (gap * inv) * ((den + num) * inv)


def col_shift(x, step):
    if step == 0:
        return x
    rows = x.shape[0]
    return pltpu.roll(x.astype(F32), (-step) % rows, 0).astype(BF16)


def row_shift(x, step):
    if step == 0:
        return x
    if step > 0:
        return jnp.concatenate([x[step:], x[:step]], axis=0)
    return jnp.concatenate([x[step:], x[: x.shape[0] + step]], axis=0)


def masked(x, lane_mask):
    reps = x.shape[1] // 128
    return x * jnp.concatenate([lane_mask] * reps, axis=1)


def tap_weight(w_ref, tap):
    w = w_ref[:, tap]
    return w.reshape(w.shape[0] * w.shape[1], w.shape[2])


def down_weight(direct_ref, spread_ref, tap):
    taps = direct_ref.shape[1]
    if tap < taps:
        return tap_weight(direct_ref, tap)
    w = spread_ref[tap - taps]
    shards, held, half = w.shape
    own = held // 2
    sides = [w[:, k : k + own].reshape(shards * own, half) for k in (0, own)]
    return jnp.concatenate(sides, axis=1)


def column_blocks(w_ref, depth):
    if len(w_ref.shape) == 2:
        return [w_ref[...]]
    return [w_ref[k].reshape(depth, w_ref.shape[3]) for k in range(w_ref.shape[0])]


def dot_nn(a, b):
    return lax.dot_general(a, b, (((1,), (0,)), ((), ())), preferred_element_type=F32)


def dot_nt(a, b):
    return lax.dot_general(a, b, (((1,), (1,)), ((), ())), preferred_element_type=F32)


def dot_tn(a, b):
    return lax.dot_general(a, b, (((0,), (0,)), ((), ())), preferred_element_type=F32)


def mid_taps(x, side):
    cols = [col_shift(x, b - 1) for b in range(3)]
    for tap in range(9):
        a, b = divmod(tap, 3)
        yield tap, row_shift(cols[b], side * (a - 1))


def down_taps(phase, side):
    cols = {}
    for pr in range(2):
        for b in range(3):
            x = phase(2 * pr + int(b != 1))
            cols[pr, b] = col_shift(x, -1) if b == 0 else x
    for tap in range(9):
        a, b = divmod(tap, 3)
        yield tap, row_shift(cols[int(a != 1), b], -side if a == 0 else 0)


def device_total(s_ref):
    count, _, channels = s_ref.shape
    start = jnp.zeros((2, channels), F32)
    return lax.fori_loop(0, count, lambda i, t: t + s_ref[i], start, unroll=8)


def moments(s_ref, cnt_ref):
    count = s_ref.shape[0]
    total = device_total(s_ref)
    inv_n = cnt_ref[2 * count + 1]
    mean = total[0:1] * inv_n

    def spread(i, t):
        d = s_ref[i][0:1] - cnt_ref[i] * mean
        return t + d * d * cnt_ref[count + i]

    between = lax.fori_loop(0, count, spread, jnp.zeros_like(mean), unroll=8)
    var = (total[1:2] + between) * inv_n
    return mean, var, lax.rsqrt(var + norm_eps)


def write_moments(mv_ref, mean, var, inv):
    mv_ref[0:1] = mean
    mv_ref[1:2] = var
    mv_ref[2:3] = inv
    mv_ref[3:8] = jnp.zeros((5, mean.shape[1]), F32)


def collect_moments(out, valid, acc_ref, num_ref, st_ref):
    step = pl.program_id(0)
    n = jnp.sum(valid, axis=0, keepdims=True)
    total = jnp.sum(out * valid, axis=0, keepdims=True)
    mean = total / jnp.maximum(n, 1.0)
    centred = out - mean
    squares = jnp.sum(valid * centred * centred, axis=0, keepdims=True)

    @pl.when(step == 0)
    def _():
        acc_ref[0:1] = total
        acc_ref[1:2] = squares
        num_ref[0:1] = jnp.broadcast_to(n, (1, 128))

    @pl.when(step > 0)
    def _():
        n_old = num_ref[0:1, 0:1]
        n_new = n_old + n
        old_mean = acc_ref[0:1] / jnp.maximum(n_old, 1.0)
        gap = mean - old_mean
        acc_ref[0:1] = acc_ref[0:1] + total
        acc_ref[1:2] = acc_ref[1:2] + squares + gap * gap * (n * n_old / jnp.maximum(n_new, 1.0))
        num_ref[0:1] = jnp.broadcast_to(n_new, (1, 128))

    @pl.when(step == pl.num_programs(0) - 1)
    def _():
        st_ref[...] = jnp.broadcast_to(acc_ref[0:2][None], st_ref.shape)


def collect_sums(g, xhat, acc_ref, st_ref):
    step = pl.program_id(0)
    first = jnp.sum(g, axis=0, keepdims=True)
    second = jnp.sum(g * xhat, axis=0, keepdims=True)

    @pl.when(step == 0)
    def _():
        acc_ref[0:1] = first
        acc_ref[1:2] = second

    @pl.when(step > 0)
    def _():
        acc_ref[0:1] = acc_ref[0:1] + first
        acc_ref[1:2] = acc_ref[1:2] + second

    @pl.when(step == pl.num_programs(0) - 1)
    def _():
        st_ref[...] = jnp.broadcast_to(acc_ref[0:2][None], st_ref.shape)


def prep_kernel(side, centre_ref, x_ref, ph_ref, down_ref, back_ref, mid_ref):
    half = ph_ref.shape[1]
    p = lax.broadcasted_iota(jnp.int32, (half, 2 * half), 0)
    s = lax.broadcasted_iota(jnp.int32, (half, 2 * half), 1)
    for pr in range(2):
        x = x_ref[0, :, pr]
        x = x.reshape(2 * half, x.shape[-1])
        for pc in range(2):
            pick = jnp.where(s == 2 * p + pc, 1.0, 0.0).astype(BF16)
            ph_ref[2 * pr + pc] = dot_nn(pick, x).astype(BF16)

    image = pl.program_id(0)
    pixel = lax.broadcasted_iota(jnp.int32, (half, 128), 0)
    spots = (pixel // side, pixel % side)
    centre = (centre_ref[image, 0], centre_ref[image, 1])

    def inside(own, other, middle, extent):
        same = (other >= middle) == (own >= middle)
        return jnp.where(same & (other >= 0) & (other < extent), 1.0, 0.0)

    down, back, mid = [], [], []
    for axis in range(2):
        at, middle = spots[axis], centre[axis]
        down.append([inside(2 * at, 2 * at + a - 1, middle, 2 * side) for a in range(3)])
        mid.append([inside(2 * at, 2 * (at + a - 1), middle, 2 * side) for a in range(3)])
        moved = []
        for a in range(3):
            to = at + int(a == 0)
            hit = inside(2 * to, 2 * to + a - 1, middle, 2 * side)
            moved.append(jnp.where(to < side, hit, 0.0))
        back.append(moved)
    for ref, parts in ((down_ref, down), (back_ref, back), (mid_ref, mid)):
        for tap in range(9):
            a, b = divmod(tap, 3)
            ref[tap] = (parts[0][a] * parts[1][b]).astype(BF16)


def first_kernel(
    side, ph_ref, m_ref, valid_ref, wa_ref, wb_ref, z_ref, st_ref, acc_ref, num_ref
):
    out = None
    for tap, x in down_taps(lambda k: ph_ref[k], side):
        part = dot_nn(masked(x, m_ref[tap]), down_weight(wa_ref, wb_ref, tap))
        out = part if out is None else out + part
    z_ref[...] = out
    collect_moments(out, valid_ref[...], acc_ref, num_ref, st_ref)


def forward_kernel(kind, side, z_ref, s_ref, cnt_ref, gain_ref, bias_ref, valid_ref, w_ref, *rest):
    rest = list(rest)
    m_ref = rest.pop(0) if kind == "three" else None
    other_ref = rest.pop(0) if kind in ("resid", "join") else None
    v_ref = rest.pop(0)
    keep_ref = rest.pop(0) if kind in ("split", "resid") else None
    mv_ref, out_ref, st_ref, acc_ref, num_ref = rest
    mean, var, inv = moments(s_ref, cnt_ref)

    @pl.when(pl.program_id(0) == 0)
    def _():
        write_moments(mv_ref, mean, var, inv)

    act = mish(((z_ref[...] - mean) * inv) * gain_ref[...] + bias_ref[...])
    if kind == "split":
        half = act.shape[1] // 2
        low = act.astype(BF16)
        v_ref[...] = low
        keep_ref[...] = act[:, half:]
        v = low[:, half:]
    elif kind == "resid":
        act = other_ref[...] + act
        keep_ref[...] = act
        v = act.astype(BF16)
        v_ref[...] = v
    elif kind == "join":
        v = jnp.concatenate([other_ref[...], act.astype(BF16)], axis=1)
        v_ref[...] = v
    else:
        v = act.astype(BF16)
        v_ref[...] = v
    if kind == "three":
        out = None
        for tap, x in mid_taps(v, side):
            part = dot_nn(masked(x, m_ref[tap]), tap_weight(w_ref, tap))
            out = part if out is None else out + part
    else:
        outs = [dot_nn(v, w) for w in column_blocks(w_ref, v.shape[1])]
        out = outs[0] if len(outs) == 1 else jnp.concatenate(outs, axis=1)
    out_ref[...] = out
    collect_moments(out, valid_ref[...], acc_ref, num_ref, st_ref)


def top_kernel(
    z_ref, s_ref, cnt_ref, gain_ref, bias_ref, cot_ref, o_ref, mv_ref, g_ref, st_ref, acc_ref
):
    mean, var, inv = moments(s_ref, cnt_ref)

    @pl.when(pl.program_id(0) == 0)
    def _():
        write_moments(mv_ref, mean, var, inv)

    xhat = (z_ref[...] - mean) * inv
    act, slope = mish_both(xhat * gain_ref[...] + bias_ref[...])
    o_ref[...] = act.astype(BF16)
    g = cot_ref[...].astype(F32) * slope
    g_ref[...] = g
    collect_sums(g, xhat, acc_ref, st_ref)


def norm_grad(g_ref, z_ref, mv_ref, s_ref, gain_ref, valid_ref, cnt_ref, tot_ref):
    total = device_total(s_ref)

    @pl.when(pl.program_id(0) == 0)
    def _():
        tot_ref[0:2] = total
        tot_ref[2:8] = jnp.zeros((6, total.shape[1]), F32)

    inv = mv_ref[2:3]
    inv_n = cnt_ref[2 * s_ref.shape[0] + 1]
    xhat = (z_ref[...] - mv_ref[0:1]) * inv
    mean_part = (valid_ref[...] * inv_n) * (total[0:1] + xhat * total[1:2])
    return (gain_ref[...] * inv * (g_ref[...] - mean_part)).astype(BF16)


def backward_kernel(
    kind,
    side,
    depth,
    g_ref,
    z_ref,
    mv_ref,
    s_ref,
    gain_ref,
    valid_ref,
    cnt_ref,
    w_ref,
    zp_ref,
    mvp_ref,
    gainp_ref,
    biasp_ref,
    *rest,
):
    rest = list(rest)
    m_ref = rest.pop(0) if kind == "three" else None
    add_ref = rest.pop(0) if kind in ("add", "merge") else None
    route_ref = rest.pop(0) if kind == "merge" else None
    dz_ref, tot_ref = rest.pop(0), rest.pop(0)
    keep_ref = rest.pop(0) if kind in ("part", "keep", "add") else None
    gp_ref, st_ref, acc_ref = rest
    dz = norm_grad(g_ref, z_ref, mv_ref, s_ref, gain_ref, valid_ref, cnt_ref, tot_ref)
    dz_ref[...] = dz
    if kind == "three":
        ga = None
        for tap, x in mid_taps(dz, side):
            part = dot_nt(masked(x, m_ref[tap]), tap_weight(w_ref, 8 - tap))
            ga = part if ga is None else ga + part
    else:
        ga, at = None, 0
        for w in column_blocks(w_ref, depth):
            part = dot_nt(dz[:, at : at + w.shape[1]], w)
            ga = part if ga is None else ga + part
            at += w.shape[1]
    if kind == "part":
        half = ga.shape[1] // 2
        keep_ref[...] = ga[:, :half]
        ga = ga[:, half:]
    elif kind == "keep":
        keep_ref[...] = ga
    elif kind == "add":
        ga = ga + add_ref[...]
        keep_ref[...] = ga
    elif kind == "merge":
        ga = jnp.concatenate([route_ref[...], ga + add_ref[...]], axis=1)
    xhat = (zp_ref[...] - mvp_ref[0:1]) * mvp_ref[2:3]
    gp = ga * mish_slope(xhat * gainp_ref[...] + biasp_ref[...])
    gp_ref[...] = gp
    collect_sums(gp, xhat, acc_ref, st_ref)


def last_norm_kernel(
    g_ref, z_ref, mv_ref, s_ref, gain_ref, valid_ref, cnt_ref, dz_ref, tot_ref
):
    dz_ref[...] = norm_grad(g_ref, z_ref, mv_ref, s_ref, gain_ref, valid_ref, cnt_ref, tot_ref)


def input_grad_kernel(side, dz_ref, m_ref, wa_ref, wb_ref, o_ref):
    dz = dz_ref[...]
    rows = dz.shape[0]
    moved = {}
    for dj in range(2):
        base = col_shift(dz, dj)
        for di in range(2):
            moved[di, dj] = row_shift(base, side * di)
    s = lax.broadcasted_iota(jnp.int32, (2 * rows, 2 * rows), 0)
    k = lax.broadcasted_iota(jnp.int32, (2 * rows, 2 * rows), 1)
    source = jnp.where(k < rows, 2 * k, 2 * (k - rows) + 1)
    put = jnp.where(s == source, 1.0, 0.0).astype(BF16)
    choices = (((1, 0),), ((2, 0), (0, 1)))
    for pr in range(2):
        both = []
        for pc in range(2):
            total = None
            for a, di in choices[pr]:
                for b, dj in choices[pc]:
                    tap = 3 * a + b
                    w = down_weight(wa_ref, wb_ref, tap)
                    part = dot_nt(masked(moved[di, dj], m_ref[tap]), w)
                    total = part if total is None else total + part
            both.append(total.astype(BF16))
        out = dot_nn(put, jnp.concatenate(both, axis=0)).astype(BF16)
        o_ref[0, :, pr] = out.reshape(side, 2 * side, out.shape[1])


def weight_grad_kernel(stride, side, first, x_ref, m_ref, dz_ref, o_ref):
    dz = dz_ref[...]
    by_shard = len(o_ref.shape) == 4
    count = o_ref.shape[1] if by_shard else o_ref.shape[0]
    taps = mid_taps(x_ref[...], side) if stride == 1 else down_taps(lambda k: x_ref[k], side)
    for tap, x in taps:
        if not first <= tap < first + count:
            continue
        grad = dot_tn(masked(x, m_ref[tap]), dz).astype(BF16)
        if by_shard:
            grad = grad.reshape(o_ref.shape[0], o_ref.shape[2], o_ref.shape[3])
            o_ref[:, tap - first] = grad
        else:
            o_ref[tap - first] = grad


def per_device(
    segment_input,
    cotangent,
    tile_centres,
    valid_mask,
    w_down,
    w_split,
    w_reduce,
    w_spread,
    w_trans,
    w_unite,
    bn_gain,
    bn_bias,
    running_mean,
    running_var,
):
    images, side, _, width = cotangent.shape
    half = w_trans.shape[2]
    c_prev = segment_input.shape[3]
    blocks = w_reduce.shape[0]
    per_image = side * side
    pixels = images * per_image
    fsdp = lax.axis_size("fsdp")
    devices = lax.axis_size("dp") * fsdp
    steps = images
    rows = pixels // steps

    def gather(shard):
        return lax.all_gather(shard, "fsdp", axis=0, tiled=False)

    groups = lax.axis_size("dp")
    taps = 9 - groups
    down = w_down.transpose(1, 0, 2)
    halves = [down[taps:, :, k : k + half] for k in range(0, width, half)]
    units = [w_split[:, 0, k : k + half] for k in range(0, width, half)]
    units += [w_reduce[b, :, 0] for b in range(blocks)] + [w_trans[:, 0]]
    units.append(jnp.zeros_like(w_trans[:, 0]))
    early = jnp.concatenate(units, axis=0).reshape(groups, -1, half)
    quarters = jnp.concatenate([*halves, early], axis=1)
    own_quarter = lax.dynamic_index_in_dim(quarters, lax.axis_index("dp"), 0, keepdims=False)
    quarter = gather(own_quarter)
    full_down = gather(lax.optimization_barrier((down[:taps], own_quarter))[0])
    tap_rows = 2 * down.shape[1]
    narrow_rows = w_trans.shape[0]
    split_rows = 2 * w_split.shape[0]

    group = lax.axis_index("dp")

    def to_group(x, k):
        return lax.ppermute(x, "dp", [(i, i ^ k) for i in range(groups)])

    def send_to_groups(piece):
        return [to_group(piece, k) for k in range(1, groups)]

    def in_order(piece, received):
        held = jnp.zeros((groups, *piece.shape), piece.dtype)
        for k, got in enumerate([piece, *received]):
            held = lax.dynamic_update_index_in_dim(held, got, group ^ k, 0)
        return held

    def deal(parts):
        held = [lax.dynamic_index_in_dim(parts, group ^ k, 0, False) for k in range(groups)]
        return held, [to_group(held[k], k) for k in range(1, groups)]

    def add_parts(own, received):
        total = own.astype(F32)
        for got in received:
            total = total + got.astype(F32)
        return total.astype(BF16)

    full_spread = [gather(w_spread[b].transpose(1, 0, 2)) for b in range(blocks)]
    full_unite = lax.all_gather(w_unite[:, 0], "fsdp", axis=0, tiled=True)

    valid = valid_mask.astype(F32).reshape(pixels, 1)
    own_count = jnp.broadcast_to(jnp.sum(valid), (devices, 1, 128))
    counts = lax.all_to_all(own_count, ALL, 0, 0, tiled=True)[:, 0, 0]
    whole_count = jnp.sum(counts)
    cnt = jnp.concatenate(
        [counts, 1.0 / jnp.maximum(counts, 1.0), jnp.stack([whole_count, 1.0 / whole_count])]
    )

    def exchange(st):
        return lax.all_to_all(st, ALL, 0, 0, tiled=True)

    smem = pl.BlockSpec(memory_space=pltpu.SMEM)

    def fixed(shape):
        return pl.BlockSpec(shape, lambda i: (0,) * len(shape))

    def single(shape, index=None):
        index = index or (0,) * len(shape)
        return pl.BlockSpec(shape, lambda i: index, pipeline_mode=pl.Buffered(1))

    def tall(channels, column=0):
        return pl.BlockSpec((rows, channels), lambda i: (i, column))

    mask_spec = pl.BlockSpec((9, rows, 128), lambda i: (0, i, 0))
    valid_spec = pl.BlockSpec((rows, 1), lambda i: (i, 0))

    def shaped(shape, dtype):
        return jax.ShapeDtypeStruct(shape, dtype)

    def stat_shape(channels):
        return shaped((devices, 2, channels), F32)

    widths = [width, width] + [half] * (2 * blocks) + [half, width]
    starts = [sum(widths[:i]) for i in range(len(widths))]
    gains = [bn_gain[s : s + c].reshape(1, c) for s, c in zip(starts, widths)]
    biases = [bn_bias[s : s + c].reshape(1, c) for s, c in zip(starts, widths)]
    layers = len(widths)

    def narrow_spec(k):
        return single((1, fsdp, narrow_rows, half), (2 + k // 2, 0, k % 2, 0))

    weights = [None] * layers
    weights[0] = (full_down, single(full_down.shape))
    for b in range(blocks):
        weights[3 + 2 * b] = (full_spread[b], single(full_spread[b].shape))
    weights[layers - 1] = (full_unite, single(full_unite.shape))

    x6 = segment_input.reshape(images, side, 2, 2 * side, c_prev)
    mask_shape = shaped((9, pixels, 128), BF16)
    mask_block = pl.BlockSpec((9, per_image, 128), lambda i: (0, i, 0))
    phases, mask_down, mask_back, mask_mid = pl.pallas_call(
        functools.partial(prep_kernel, side),
        grid=(images,),
        in_specs=[
            pl.BlockSpec(memory_space=pltpu.SMEM),
            pl.BlockSpec((1, side, 2, 2 * side, c_prev), lambda i: (i, 0, 0, 0, 0)),
        ],
        out_specs=[
            pl.BlockSpec((4, per_image, c_prev), lambda i: (0, i, 0)),
            mask_block,
            mask_block,
            mask_block,
        ],
        out_shape=[shaped((4, pixels, c_prev), BF16), mask_shape, mask_shape, mask_shape],
        compiler_params=params(),
        cost_estimate=cost(0, 5 * pixels * c_prev),
        name="parity_images",
    )(tile_centres, x6)
    quarter, phases, mask_down, mask_back, mask_mid, cnt = lax.optimization_barrier(
        (quarter, phases, mask_down, mask_back, mask_mid, cnt)
    )
    piece = quarter[:, :tap_rows]
    down_rest = in_order(piece, send_to_groups(piece))
    early_piece = lax.optimization_barrier((quarter[:, tap_rows:], down_rest))[0]
    early_got = send_to_groups(early_piece)

    def scratch(channels):
        return [pltpu.VMEM((8, channels), F32), pltpu.VMEM((8, 128), F32)]

    z, st = [None] * layers, [None] * layers
    z[0], st[0] = pl.pallas_call(
        functools.partial(first_kernel, side),
        grid=(steps,),
        in_specs=[
            pl.BlockSpec((4, rows, c_prev), lambda i: (0, i, 0)),
            mask_spec,
            valid_spec,
            weights[0][1],
            single(down_rest.shape),
        ],
        out_specs=[tall(width), fixed((devices, 2, width))],
        out_shape=[shaped((pixels, width), F32), stat_shape(width)],
        scratch_shapes=scratch(width),
        compiler_params=params(),
        cost_estimate=cost(9 * pixels * c_prev * width, 6 * pixels * width),
        name="down_forward",
    )(phases, mask_down, valid, full_down, down_rest)

    *early_got, first_gathered = lax.optimization_barrier((*early_got, exchange(st[0])))
    early = in_order(early_piece, early_got)
    weights[1] = (early, single((2, *early.shape[1:]), (0, 0, 0, 0)))
    for k, layer in enumerate([2 + 2 * b for b in range(blocks)] + [layers - 2]):
        weights[layer] = (early, narrow_spec(k))

    inputs = [None] * layers
    moment = [None] * layers

    def forward(layer, kind, extra=(), extra_specs=(), gathered=None):
        prev, channels = layer - 1, widths[layer - 1]
        w, w_spec = weights[layer]
        if gathered is None:
            gathered = exchange(st[prev])
        args = [z[prev], gathered, cnt, gains[prev], biases[prev], valid, w, *extra]
        specs = [
            tall(channels),
            fixed((devices, 2, channels)),
            smem,
            fixed((1, channels)),
            fixed((1, channels)),
            valid_spec,
            w_spec,
            *extra_specs,
        ]
        v_width = 2 * half if kind == "join" else channels
        out_specs, out_shape = [tall(v_width)], [shaped((pixels, v_width), BF16)]
        if kind in ("split", "resid"):
            out_specs.append(tall(half))
            out_shape.append(shaped((pixels, half), F32))
        n = widths[layer]
        out_specs += [fixed((8, channels)), tall(n), fixed((devices, 2, n))]
        out_shape += [shaped((8, channels), F32), shaped((pixels, n), F32), stat_shape(n)]
        outs = list(
            pl.pallas_call(
                functools.partial(forward_kernel, kind, side),
                grid=(steps,),
                in_specs=specs,
                out_specs=out_specs,
                out_shape=out_shape,
                scratch_shapes=scratch(n),
                compiler_params=params(),
                cost_estimate=cost(9 * pixels * half * half * int(kind == "three"), 8 * pixels * half + 4 * pixels * channels),
                name="forward_" + kind,
            )(*args)
        )
        inputs[layer] = outs.pop(0)
        keep = outs.pop(0) if kind in ("split", "resid") else None
        moment[prev], z[layer], st[layer] = outs
        return keep

    forward(1, "plain", gathered=first_gathered)
    stream = None
    for b in range(blocks):
        if b == 0:
            stream = forward(2, "split")
        else:
            stream = forward(2 + 2 * b, "resid", (stream,), (tall(half),))
        forward(3 + 2 * b, "three", (mask_mid,), (mask_spec,))
    forward(layers - 2, "resid", (stream,), (tall(half),))
    split_low = inputs[2]
    forward(layers - 1, "join", (split_low,), (tall(half),))

    last = layers - 1
    n = widths[last]
    output, moment[last], g, st_back = pl.pallas_call(
        top_kernel,
        grid=(steps,),
        in_specs=[
            tall(n),
            fixed((devices, 2, n)),
            smem,
            fixed((1, n)),
            fixed((1, n)),
            tall(n),
        ],
        out_specs=[tall(n), fixed((8, n)), tall(n), fixed((devices, 2, n))],
        out_shape=[
            shaped((pixels, n), BF16),
            shaped((8, n), F32),
            shaped((pixels, n), F32),
            stat_shape(n),
        ],
        scratch_shapes=[pltpu.VMEM((8, n), F32)],
        compiler_params=params(),
        cost_estimate=cost(0, 8 * pixels * n),
        name="top",
    )(z[last], exchange(st[last]), cnt, gains[last], biases[last], cotangent.reshape(pixels, n))

    totals = [None] * layers
    dz = [None] * layers

    def backward(layer, kind, g, gathered, extra=(), extra_specs=()):
        prev, channels = layer - 1, widths[layer]
        cp = widths[prev]
        w, w_spec = weights[layer]
        depth = 2 * half if kind == "part" else (half if kind == "merge" else cp)
        args = [g, z[layer], moment[layer], gathered, gains[layer], valid, cnt, w]
        args += [z[prev], moment[prev], gains[prev], biases[prev], *extra]
        specs = [
            tall(channels),
            tall(channels),
            fixed((8, channels)),
            fixed((devices, 2, channels)),
            fixed((1, channels)),
            valid_spec,
            smem,
            w_spec,
            tall(cp),
            fixed((8, cp)),
            fixed((1, cp)),
            fixed((1, cp)),
            *extra_specs,
        ]
        out_specs = [tall(channels), fixed((8, channels))]
        out_shape = [shaped((pixels, channels), BF16), shaped((8, channels), F32)]
        if kind in ("part", "keep", "add"):
            out_specs.append(tall(half))
            out_shape.append(shaped((pixels, half), F32))
        out_specs += [tall(cp), fixed((devices, 2, cp))]
        out_shape += [shaped((pixels, cp), F32), stat_shape(cp)]
        outs = list(
            pl.pallas_call(
                functools.partial(backward_kernel, kind, side, depth),
                grid=(steps,),
                in_specs=specs,
                out_specs=out_specs,
                out_shape=out_shape,
                scratch_shapes=[pltpu.VMEM((8, cp), F32)],
                compiler_params=params(),
                cost_estimate=cost(9 * pixels * half * half * int(kind == "three"), 8 * pixels * half + 4 * pixels * cp),
                name="backward_" + kind,
            )(*args)
        )
        dz[layer], totals[layer] = outs.pop(0), outs.pop(0)
        keep = outs.pop(0) if kind in ("part", "keep", "add") else None
        return outs[0], outs[1], keep

    def tap_grad(stride, x, lane_mask, dz_low, w_shape, first=0):
        return pl.pallas_call(
            functools.partial(weight_grad_kernel, stride, side, first),
            out_shape=shaped(w_shape, BF16),
            compiler_params=params(),
            cost_estimate=cost(9 * pixels * half * dz_low.shape[1], 2 * pixels * dz_low.shape[1]),
            name="weight_grad_" + str(stride),
        )(x, lane_mask, dz_low)

    def flat_grad(x, dz_low):
        return jnp.einsum("pk,pn->kn", x, dz_low, preferred_element_type=F32).astype(BF16)

    def scatter(grad):
        return lax.psum_scatter(grad, "fsdp", scatter_dimension=0, tiled=True)

    def sum_own_part(own):
        parts = own.reshape(groups, own.shape[0] // groups, own.shape[1])
        parts = lax.all_to_all(parts, "dp", 0, 0, tiled=True)
        return jnp.sum(parts.astype(F32), axis=0).astype(BF16)

    def give_back(part):
        sent = jnp.broadcast_to(part[None], (groups, *part.shape))
        return lax.all_to_all(sent, "dp", 0, 0, tiled=True).astype(F32)

    def beside(st_back, grad, *due):
        return lax.optimization_barrier((exchange(st_back), grad, *due))[:2]

    g, st_back, grad_route = backward(last, "part", g, exchange(st_back))
    grad_unite = flat_grad(inputs[last], dz[last])
    gathered, grad_unite = beside(st_back, grad_unite)
    own_unite = scatter(grad_unite)
    g, st_back, grad_stream = backward(last - 1, "keep", g, gathered)
    narrow_grads = [None] * (blocks + 1)
    narrow_grads[blocks] = flat_grad(inputs[last - 1], dz[last - 1])
    gathered, narrow_grads[blocks] = beside(st_back, narrow_grads[blocks])
    own_spread = [None] * blocks
    for b in reversed(range(blocks)):
        layer = 3 + 2 * b
        g, st_back, _ = backward(layer, "three", g, gathered, (mask_mid,), (mask_spec,))
        own = tap_grad(1, inputs[layer], mask_mid, dz[layer], full_spread[b].shape)
        due = (own_unite,) if b == blocks - 1 else ()
        gathered, own = beside(st_back, own, *due)
        own_spread[b] = scatter(own)
        layer = 2 + 2 * b
        if b > 0:
            g, st_back, grad_stream = backward(
                layer, "add", g, gathered, (grad_stream,), (tall(half),)
            )
            low = inputs[layer]
        else:
            g, st_back, _ = backward(
                layer, "merge", g, gathered, (grad_stream, grad_route), (tall(half), tall(half))
            )
            low = inputs[layer][:, half:]
        narrow_grads[b] = flat_grad(low, dz[layer])
        due = own_spread[1:2] if b == 0 else ()
        gathered, narrow_grads[b] = beside(st_back, narrow_grads[b], *due)
    g, st_back, _ = backward(1, "plain", g, gathered)
    split_grads = [flat_grad(inputs[1], dz[1][:, k : k + half]) for k in range(0, width, half)]
    late = [w.reshape(fsdp, -1, half) for w in (*split_grads, *narrow_grads)]
    gathered, grad_late = beside(st_back, jnp.concatenate(late, axis=1))
    own_late = scatter(grad_late)[0]
    dz[0], totals[0] = pl.pallas_call(
        last_norm_kernel,
        grid=(steps,),
        in_specs=[
            tall(width),
            tall(width),
            fixed((8, width)),
            fixed((devices, 2, width)),
            fixed((1, width)),
            valid_spec,
            smem,
        ],
        out_specs=[tall(width), fixed((8, width))],
        out_shape=[shaped((pixels, width), BF16), shaped((8, width), F32)],
        compiler_params=params(),
        cost_estimate=cost(0, 5 * pixels * width),
        name="down_norm",
    )(g, z[0], moment[0], gathered, gains[0], valid, cnt)
    direct = tap_grad(2, phases, mask_down, dz[0], full_down.shape)
    own_direct = scatter(direct)
    dz_low = lax.optimization_barrier((dz[0], direct, own_spread[0]))[0]
    rest = tap_grad(2, phases, mask_down, dz_low, (groups, c_prev, width), taps)
    first_packed = lax.optimization_barrier((*own_spread, own_unite, direct))[:-1]
    first_packed = [o.reshape(-1, half) for o in first_packed]
    first_part = sum_own_part(jnp.concatenate(first_packed, axis=0))
    first_part, rest = lax.optimization_barrier((first_part, rest))
    rest_held, rest_got = deal(rest)
    *rest_held, dz_low = lax.optimization_barrier((*rest_held, dz_low))
    input_grad = pl.pallas_call(
        functools.partial(input_grad_kernel, side),
        grid=(images,),
        in_specs=[
            pl.BlockSpec((per_image, width), lambda i: (i, 0)),
            pl.BlockSpec((9, per_image, 128), lambda i: (0, i, 0)),
            weights[0][1],
            single(down_rest.shape),
        ],
        out_specs=pl.BlockSpec((1, side, 2, 2 * side, c_prev), lambda i: (i, 0, 0, 0, 0)),
        out_shape=shaped(x6.shape, BF16),
        compiler_params=params(),
        cost_estimate=cost(9 * pixels * c_prev * width, 8 * pixels * width),
        name="input_grad",
    )(dz_low, mask_back, full_down, down_rest).reshape(segment_input.shape)

    *received, input_grad = lax.optimization_barrier((*rest_got, input_grad))
    rest_sum = add_parts(rest_held[0], received)
    own_rest = scatter(rest_sum)
    *totals, rest_sum = lax.optimization_barrier((*totals, rest_sum))
    *moment, rest_sum = lax.optimization_barrier((*moment, rest_sum))
    first_part = lax.optimization_barrier((first_part, rest_sum))[0]
    first_sums = give_back(first_part).reshape(-1, half)
    own_late, own_direct, first_sums = lax.optimization_barrier((own_late, own_direct, first_sums))
    second = [own_late, own_direct.reshape(-1, width)]
    cut = [o.reshape(groups, -1, o.shape[-1]) for o in second]
    cut[1] = cut[1].reshape(groups, -1, half)
    second_part = sum_own_part(jnp.concatenate(cut, axis=1).reshape(-1, half))
    late_rows = own_late.shape[0]
    late_own = late_rows // groups
    sums = give_back(second_part)
    grad_direct = sums[:, late_own:].reshape(own_direct.shape[1:])
    late_sums = sums[:, :late_own].reshape(-1, half)
    spread_rows = first_packed[0].shape[0]
    split_parts = late_sums[:split_rows].reshape(-1, split_rows // 2, half)
    grad_split = jnp.concatenate([split_parts[0], split_parts[1]], axis=1)
    narrow = late_sums[split_rows:].reshape(blocks + 1, narrow_rows, 1, half)
    grad_spread = first_sums[: blocks * spread_rows]
    grad_spread = grad_spread.reshape(blocks, 9, narrow_rows, half).transpose(0, 2, 1, 3)
    grad_unite = first_sums[blocks * spread_rows :].reshape(own_unite.shape)[:, None]
    grad_split, narrow, grad_spread, grad_unite, grad_direct, own_rest = lax.optimization_barrier(
        (grad_split, narrow, grad_spread, grad_unite, grad_direct, own_rest)
    )
    grad_down = jnp.concatenate([grad_direct, give_back(own_rest)], axis=0).transpose(1, 0, 2)

    means = jnp.concatenate([m[0] for m in moment])
    variances = jnp.concatenate([m[1] for m in moment])
    new_mean = (1.0 - momentum_rate) * running_mean + momentum_rate * means
    new_var = (1.0 - momentum_rate) * running_var + momentum_rate * variances * whole_count / (
        whole_count - 1.0
    )
    return (
        output.reshape(cotangent.shape),
        input_grad,
        grad_down,
        grad_split[:, None],
        narrow[:blocks],
        grad_spread,
        narrow[blocks],
        grad_unite,
        jnp.concatenate([t[1] for t in totals]),
        jnp.concatenate([t[0] for t in totals]),
        new_mean,
        new_var,
    )


def solution(mesh):
    image = P(ALL, None, None, None)
    row3 = P("fsdp", None, None)
    row4 = P(None, "fsdp", None, None)
    return jax.shard_map(
        per_device,
        mesh=mesh,
        in_specs=(
            image,
            image,
            P(ALL, None),
            P(ALL, None, None),
            row3,
            row3,
            row4,
            row4,
            row3,
            row3,
            P(),
            P(),
            P(),
            P(),
        ),
        out_specs=(image, image, row3, row3, row4, row4, row3, row3, P(), P(), P(), P()),
        check_vma=False,
    )
```

```python
import functools

import jax
import jax.numpy as jnp
from jax import lax
from jax.experimental import pallas as pl
from jax.experimental.pallas import tpu as pltpu
from jax.sharding import PartitionSpec as P

norm_eps = 1e-05
momentum_rate = 0.1
ALL = ("dp", "fsdp")
F32 = jnp.float32
BF16 = jnp.bfloat16
VMEM_LIMIT = 58 * 1024 * 1024


def params():
    return pltpu.CompilerParams(vmem_limit_bytes=VMEM_LIMIT)


def cost(products, elements):
    return pl.CostEstimate(flops=2 * products, transcendentals=0, bytes_accessed=4 * elements)


def mish_parts(y):
    e = jnp.exp(jnp.minimum(y, 20.0))
    n = e * (e + 2.0)
    return e, n, 1.0 / (n + 2.0)


def mish(y):
    _, n, r = mish_parts(y)
    return y * (n * r)


def mish_slope(y):
    e, n, r = mish_parts(y)
    return r * (n + (4.0 * y) * ((n - e) * r))


def mish_both(y):
    e, n, r = mish_parts(y)
    return y * (n * r), r * (n + (4.0 * y) * ((n - e) * r))


def col_shift(x, step):
    if step == 0:
        return x
    rows = x.shape[0]
    return pltpu.roll(x.astype(F32), (-step) % rows, 0).astype(BF16)


def row_shift(x, step):
    if step == 0:
        return x
    if step > 0:
        return jnp.concatenate([x[step:], x[:step]], axis=0)
    return jnp.concatenate([x[step:], x[: x.shape[0] + step]], axis=0)


def masked(x, lane_mask):
    reps = x.shape[1] // 128
    return x * jnp.concatenate([lane_mask] * reps, axis=1)


def tap_weight(w_ref, tap):
    w = w_ref[:, tap]
    return w.reshape(w.shape[0] * w.shape[1], w.shape[2])


def down_weight(direct_ref, spread_ref, tap):
    taps = direct_ref.shape[1]
    if tap < taps:
        return tap_weight(direct_ref, tap)
    w = spread_ref[tap - taps]
    shards, held, half = w.shape
    own = held // 2
    sides = [w[:, k : k + own].reshape(shards * own, half) for k in (0, own)]
    return jnp.concatenate(sides, axis=1)


def column_blocks(w_ref, depth):
    if len(w_ref.shape) == 2:
        return [w_ref[...]]
    return [w_ref[k].reshape(depth, w_ref.shape[3]) for k in range(w_ref.shape[0])]


def dot_nn(a, b):
    return lax.dot_general(a, b, (((1,), (0,)), ((), ())), preferred_element_type=F32)


def dot_nt(a, b):
    return lax.dot_general(a, b, (((1,), (1,)), ((), ())), preferred_element_type=F32)


def dot_tn(a, b):
    return lax.dot_general(a, b, (((0,), (0,)), ((), ())), preferred_element_type=F32)


def mid_taps(x, side):
    cols = [col_shift(x, b - 1) for b in range(3)]
    for tap in range(9):
        a, b = divmod(tap, 3)
        yield tap, row_shift(cols[b], side * (a - 1))


def down_taps(phase, side):
    cols = {}
    for pr in range(2):
        for b in range(3):
            x = phase(2 * pr + int(b != 1))
            cols[pr, b] = col_shift(x, -1) if b == 0 else x
    for tap in range(9):
        a, b = divmod(tap, 3)
        yield tap, row_shift(cols[int(a != 1), b], -side if a == 0 else 0)


def device_total(s_ref):
    count, _, channels = s_ref.shape
    start = jnp.zeros((2, channels), F32)
    return lax.fori_loop(0, count, lambda i, t: t + s_ref[i], start, unroll=8)


def moments(s_ref, cnt_ref):
    count = s_ref.shape[0]
    total = device_total(s_ref)
    inv_n = cnt_ref[2 * count + 1]
    mean = total[0:1] * inv_n

    def spread(i, t):
        d = s_ref[i][0:1] - cnt_ref[i] * mean
        return t + d * d * cnt_ref[count + i]

    between = lax.fori_loop(0, count, spread, jnp.zeros_like(mean), unroll=8)
    var = (total[1:2] + between) * inv_n
    return mean, var, lax.rsqrt(var + norm_eps)


def kept_moments(s_ref, cnt_ref, mv_ref):
    @pl.when(pl.program_id(0) == 0)
    def _():
        mean, var, inv = moments(s_ref, cnt_ref)
        mv_ref[0:1] = mean
        mv_ref[1:2] = var
        mv_ref[2:3] = inv
        mv_ref[3:8] = jnp.zeros((5, mean.shape[1]), F32)

    return mv_ref[0:1], mv_ref[2:3]


def collect_moments(out, valid, acc_ref, num_ref, st_ref):
    step = pl.program_id(0)
    n = jnp.sum(valid, axis=0, keepdims=True)
    total = jnp.sum(out * valid, axis=0, keepdims=True)
    mean = total / jnp.maximum(n, 1.0)
    centred = out - mean
    squares = jnp.sum(valid * centred * centred, axis=0, keepdims=True)

    @pl.when(step == 0)
    def _():
        acc_ref[0:1] = total
        acc_ref[1:2] = squares
        num_ref[0:1] = jnp.broadcast_to(n, (1, 128))

    @pl.when(step > 0)
    def _():
        n_old = num_ref[0:1, 0:1]
        n_new = n_old + n
        old_mean = acc_ref[0:1] / jnp.maximum(n_old, 1.0)
        gap = mean - old_mean
        acc_ref[0:1] = acc_ref[0:1] + total
        acc_ref[1:2] = acc_ref[1:2] + squares + gap * gap * (n * n_old / jnp.maximum(n_new, 1.0))
        num_ref[0:1] = jnp.broadcast_to(n_new, (1, 128))

    @pl.when(step == pl.num_programs(0) - 1)
    def _():
        st_ref[...] = jnp.broadcast_to(acc_ref[0:2][None], st_ref.shape)


def collect_sums(g, xhat, acc_ref, st_ref):
    step = pl.program_id(0)
    first = jnp.sum(g, axis=0, keepdims=True)
    second = jnp.sum(g * xhat, axis=0, keepdims=True)

    @pl.when(step == 0)
    def _():
        acc_ref[0:1] = first
        acc_ref[1:2] = second

    @pl.when(step > 0)
    def _():
        acc_ref[0:1] = acc_ref[0:1] + first
        acc_ref[1:2] = acc_ref[1:2] + second

    @pl.when(step == pl.num_programs(0) - 1)
    def _():
        st_ref[...] = jnp.broadcast_to(acc_ref[0:2][None], st_ref.shape)


def prep_kernel(side, centre_ref, x_ref, ph_ref, down_ref, back_ref, mid_ref):
    half = ph_ref.shape[1]
    p = lax.broadcasted_iota(jnp.int32, (half, 2 * half), 0)
    s = lax.broadcasted_iota(jnp.int32, (half, 2 * half), 1)
    for pr in range(2):
        x = x_ref[0, :, pr]
        x = x.reshape(2 * half, x.shape[-1])
        for pc in range(2):
            pick = jnp.where(s == 2 * p + pc, 1.0, 0.0).astype(BF16)
            ph_ref[2 * pr + pc] = dot_nn(pick, x).astype(BF16)

    image = pl.program_id(0)
    pixel = lax.broadcasted_iota(jnp.int32, (half, 128), 0)
    spots = (pixel // side, pixel % side)
    centre = (centre_ref[image, 0], centre_ref[image, 1])

    def inside(own, other, middle, extent):
        same = (other >= middle) == (own >= middle)
        return jnp.where(same & (other >= 0) & (other < extent), 1.0, 0.0)

    down, back, mid = [], [], []
    for axis in range(2):
        at, middle = spots[axis], centre[axis]
        down.append([inside(2 * at, 2 * at + a - 1, middle, 2 * side) for a in range(3)])
        mid.append([inside(2 * at, 2 * (at + a - 1), middle, 2 * side) for a in range(3)])
        moved = []
        for a in range(3):
            to = at + int(a == 0)
            hit = inside(2 * to, 2 * to + a - 1, middle, 2 * side)
            moved.append(jnp.where(to < side, hit, 0.0))
        back.append(moved)
    for ref, parts in ((down_ref, down), (back_ref, back), (mid_ref, mid)):
        for tap in range(9):
            a, b = divmod(tap, 3)
            ref[tap] = (parts[0][a] * parts[1][b]).astype(BF16)


def first_kernel(
    side, ph_ref, m_ref, valid_ref, wa_ref, wb_ref, z_ref, st_ref, acc_ref, num_ref
):
    out = None
    for tap, x in down_taps(lambda k: ph_ref[k], side):
        part = dot_nn(masked(x, m_ref[tap]), down_weight(wa_ref, wb_ref, tap))
        out = part if out is None else out + part
    z_ref[...] = out
    collect_moments(out, valid_ref[...], acc_ref, num_ref, st_ref)


def forward_kernel(kind, side, z_ref, s_ref, cnt_ref, gain_ref, bias_ref, valid_ref, w_ref, *rest):
    rest = list(rest)
    m_ref = rest.pop(0) if kind == "three" else None
    other_ref = rest.pop(0) if kind in ("resid", "join") else None
    v_ref = rest.pop(0)
    keep_ref = rest.pop(0) if kind in ("split", "resid") else None
    mv_ref, out_ref, st_ref, acc_ref, num_ref = rest
    mean, inv = kept_moments(s_ref, cnt_ref, mv_ref)
    act = mish(((z_ref[...] - mean) * inv) * gain_ref[...] + bias_ref[...])
    if kind == "split":
        half = act.shape[1] // 2
        low = act.astype(BF16)
        v_ref[...] = low
        keep_ref[...] = act[:, half:]
        v = low[:, half:]
    elif kind == "resid":
        act = other_ref[...] + act
        keep_ref[...] = act
        v = act.astype(BF16)
        v_ref[...] = v
    elif kind == "join":
        v = jnp.concatenate([other_ref[...], act.astype(BF16)], axis=1)
        v_ref[...] = v
    else:
        v = act.astype(BF16)
        v_ref[...] = v
    if kind == "three":
        out = None
        for tap, x in mid_taps(v, side):
            part = dot_nn(masked(x, m_ref[tap]), tap_weight(w_ref, tap))
            out = part if out is None else out + part
    else:
        outs = [dot_nn(v, w) for w in column_blocks(w_ref, v.shape[1])]
        out = outs[0] if len(outs) == 1 else jnp.concatenate(outs, axis=1)
    out_ref[...] = out
    collect_moments(out, valid_ref[...], acc_ref, num_ref, st_ref)


def top_kernel(
    z_ref, s_ref, cnt_ref, gain_ref, bias_ref, cot_ref, o_ref, mv_ref, g_ref, st_ref, acc_ref
):
    mean, inv = kept_moments(s_ref, cnt_ref, mv_ref)
    xhat = (z_ref[...] - mean) * inv
    act, slope = mish_both(xhat * gain_ref[...] + bias_ref[...])
    o_ref[...] = act.astype(BF16)
    g = cot_ref[...].astype(F32) * slope
    g_ref[...] = g.astype(BF16)
    collect_sums(g, xhat, acc_ref, st_ref)


def norm_grad(g_ref, z_ref, mv_ref, s_ref, gain_ref, valid_ref, cnt_ref, tot_ref):
    @pl.when(pl.program_id(0) == 0)
    def _():
        total = device_total(s_ref)
        tot_ref[0:2] = total
        tot_ref[2:8] = jnp.zeros((6, total.shape[1]), F32)

    total = tot_ref[0:2]
    inv = mv_ref[2:3]
    inv_n = cnt_ref[2 * s_ref.shape[0] + 1]
    xhat = (z_ref[...] - mv_ref[0:1]) * inv
    mean_part = (valid_ref[...] * inv_n) * (total[0:1] + xhat * total[1:2])
    return (gain_ref[...] * inv * (g_ref[...].astype(F32) - mean_part)).astype(BF16)


def backward_kernel(
    kind,
    side,
    depth,
    g_ref,
    z_ref,
    mv_ref,
    s_ref,
    gain_ref,
    valid_ref,
    cnt_ref,
    w_ref,
    zp_ref,
    mvp_ref,
    gainp_ref,
    biasp_ref,
    *rest,
):
    rest = list(rest)
    m_ref = rest.pop(0) if kind == "three" else None
    add_ref = rest.pop(0) if kind in ("add", "merge") else None
    route_ref = rest.pop(0) if kind == "merge" else None
    dz_ref, tot_ref = rest.pop(0), rest.pop(0)
    keep_ref = rest.pop(0) if kind in ("part", "keep", "add") else None
    gp_ref, st_ref, acc_ref = rest
    dz = norm_grad(g_ref, z_ref, mv_ref, s_ref, gain_ref, valid_ref, cnt_ref, tot_ref)
    dz_ref[...] = dz
    if kind == "three":
        ga = None
        for tap, x in mid_taps(dz, side):
            part = dot_nt(masked(x, m_ref[tap]), tap_weight(w_ref, 8 - tap))
            ga = part if ga is None else ga + part
    else:
        ga, at = None, 0
        for w in column_blocks(w_ref, depth):
            part = dot_nt(dz[:, at : at + w.shape[1]], w)
            ga = part if ga is None else ga + part
            at += w.shape[1]
    if kind == "part":
        half = ga.shape[1] // 2
        keep_ref[...] = ga[:, :half]
        ga = ga[:, half:]
    elif kind == "keep":
        keep_ref[...] = ga
    elif kind == "add":
        ga = ga + add_ref[...]
        keep_ref[...] = ga
    elif kind == "merge":
        ga = jnp.concatenate([route_ref[...], ga + add_ref[...]], axis=1)
    xhat = (zp_ref[...] - mvp_ref[0:1]) * mvp_ref[2:3]
    gp = ga * mish_slope(xhat * gainp_ref[...] + biasp_ref[...])
    gp_ref[...] = gp.astype(BF16)
    collect_sums(gp, xhat, acc_ref, st_ref)


def last_norm_kernel(
    g_ref, z_ref, mv_ref, s_ref, gain_ref, valid_ref, cnt_ref, dz_ref, tot_ref
):
    dz_ref[...] = norm_grad(g_ref, z_ref, mv_ref, s_ref, gain_ref, valid_ref, cnt_ref, tot_ref)


def input_grad_kernel(side, dz_ref, m_ref, wa_ref, wb_ref, o_ref):
    dz = dz_ref[...]
    rows = dz.shape[0]
    moved = {}
    for dj in range(2):
        base = col_shift(dz, dj)
        for di in range(2):
            moved[di, dj] = row_shift(base, side * di)
    s = lax.broadcasted_iota(jnp.int32, (2 * rows, 2 * rows), 0)
    k = lax.broadcasted_iota(jnp.int32, (2 * rows, 2 * rows), 1)
    source = jnp.where(k < rows, 2 * k, 2 * (k - rows) + 1)
    put = jnp.where(s == source, 1.0, 0.0).astype(BF16)
    choices = (((1, 0),), ((2, 0), (0, 1)))
    for pr in range(2):
        both = []
        for pc in range(2):
            total = None
            for a, di in choices[pr]:
                for b, dj in choices[pc]:
                    tap = 3 * a + b
                    w = down_weight(wa_ref, wb_ref, tap)
                    part = dot_nt(masked(moved[di, dj], m_ref[tap]), w)
                    total = part if total is None else total + part
            both.append(total.astype(BF16))
        out = dot_nn(put, jnp.concatenate(both, axis=0)).astype(BF16)
        o_ref[0, :, pr] = out.reshape(side, 2 * side, out.shape[1])


def weight_grad_kernel(stride, side, first, x_ref, m_ref, dz_ref, o_ref):
    dz = dz_ref[...]
    by_shard = len(o_ref.shape) == 4
    count = o_ref.shape[1] if by_shard else o_ref.shape[0]
    taps = mid_taps(x_ref[...], side) if stride == 1 else down_taps(lambda k: x_ref[k], side)
    for tap, x in taps:
        if not first <= tap < first + count:
            continue
        grad = dot_tn(masked(x, m_ref[tap]), dz).astype(BF16)
        if by_shard:
            grad = grad.reshape(o_ref.shape[0], o_ref.shape[2], o_ref.shape[3])
            o_ref[:, tap - first] = grad
        else:
            o_ref[tap - first] = grad


def per_device(
    segment_input,
    cotangent,
    tile_centres,
    valid_mask,
    w_down,
    w_split,
    w_reduce,
    w_spread,
    w_trans,
    w_unite,
    bn_gain,
    bn_bias,
    running_mean,
    running_var,
):
    images, side, _, width = cotangent.shape
    half = w_trans.shape[2]
    c_prev = segment_input.shape[3]
    blocks = w_reduce.shape[0]
    per_image = side * side
    pixels = images * per_image
    fsdp = lax.axis_size("fsdp")
    devices = lax.axis_size("dp") * fsdp
    steps = images
    rows = pixels // steps

    def gather(shard):
        return lax.all_gather(shard, "fsdp", axis=0, tiled=False)

    groups = lax.axis_size("dp")
    taps = 9 - groups
    down = w_down.transpose(1, 0, 2)
    halves = [down[taps:, :, k : k + half] for k in range(0, width, half)]
    units = [w_split[:, 0, k : k + half] for k in range(0, width, half)]
    units += [w_reduce[b, :, 0] for b in range(blocks)] + [w_trans[:, 0]]
    units.append(jnp.zeros_like(w_trans[:, 0]))
    early = jnp.concatenate(units, axis=0).reshape(groups, -1, half)
    quarters = jnp.concatenate([*halves, early], axis=1)
    own_quarter = lax.dynamic_index_in_dim(quarters, lax.axis_index("dp"), 0, keepdims=False)
    quarter = gather(own_quarter)
    full_down = gather(lax.optimization_barrier((down[:taps], own_quarter))[0])
    tap_rows = 2 * down.shape[1]
    narrow_rows = w_trans.shape[0]
    split_rows = 2 * w_split.shape[0]

    group = lax.axis_index("dp")

    def to_group(x, k):
        return lax.ppermute(x, "dp", [(i, i ^ k) for i in range(groups)])

    def send_to_groups(piece):
        return [to_group(piece, k) for k in range(1, groups)]

    def in_order(piece, received):
        held = jnp.zeros((groups, *piece.shape), piece.dtype)
        for k, got in enumerate([piece, *received]):
            held = lax.dynamic_update_index_in_dim(held, got, group ^ k, 0)
        return held

    def deal(parts):
        held = [lax.dynamic_index_in_dim(parts, group ^ k, 0, False) for k in range(groups)]
        return held, [to_group(held[k], k) for k in range(1, groups)]

    def add_parts(own, received):
        total = own.astype(F32)
        for got in received:
            total = total + got.astype(F32)
        return total.astype(BF16)

    full_spread = [gather(w_spread[b].transpose(1, 0, 2)) for b in range(blocks)]
    full_unite = lax.all_gather(w_unite[:, 0], "fsdp", axis=0, tiled=True)

    valid = valid_mask.astype(F32).reshape(pixels, 1)
    own_count = jnp.broadcast_to(jnp.sum(valid), (devices, 1, 128))
    counts = lax.all_to_all(own_count, ALL, 0, 0, tiled=True)[:, 0, 0]
    whole_count = jnp.sum(counts)
    cnt = jnp.concatenate(
        [counts, 1.0 / jnp.maximum(counts, 1.0), jnp.stack([whole_count, 1.0 / whole_count])]
    )

    def exchange(st):
        return lax.all_to_all(st, ALL, 0, 0, tiled=True)

    smem = pl.BlockSpec(memory_space=pltpu.SMEM)

    def fixed(shape):
        return pl.BlockSpec(shape, lambda i: (0,) * len(shape))

    def single(shape, index=None):
        index = index or (0,) * len(shape)
        return pl.BlockSpec(shape, lambda i: index, pipeline_mode=pl.Buffered(1))

    def tall(channels, column=0):
        return pl.BlockSpec((rows, channels), lambda i: (i, column))

    mask_spec = pl.BlockSpec((9, rows, 128), lambda i: (0, i, 0))
    valid_spec = pl.BlockSpec((rows, 1), lambda i: (i, 0))

    def shaped(shape, dtype):
        return jax.ShapeDtypeStruct(shape, dtype)

    def stat_shape(channels):
        return shaped((devices, 2, channels), F32)

    widths = [width, width] + [half] * (2 * blocks) + [half, width]
    starts = [sum(widths[:i]) for i in range(len(widths))]
    gains = [bn_gain[s : s + c].reshape(1, c) for s, c in zip(starts, widths)]
    biases = [bn_bias[s : s + c].reshape(1, c) for s, c in zip(starts, widths)]
    layers = len(widths)

    def narrow_spec(k):
        return single((1, fsdp, narrow_rows, half), (2 + k // 2, 0, k % 2, 0))

    weights = [None] * layers
    weights[0] = (full_down, single(full_down.shape))
    for b in range(blocks):
        weights[3 + 2 * b] = (full_spread[b], single(full_spread[b].shape))
    weights[layers - 1] = (full_unite, single(full_unite.shape))

    x6 = segment_input.reshape(images, side, 2, 2 * side, c_prev)
    mask_shape = shaped((9, pixels, 128), BF16)
    mask_block = pl.BlockSpec((9, per_image, 128), lambda i: (0, i, 0))
    phases, mask_down, mask_back, mask_mid = pl.pallas_call(
        functools.partial(prep_kernel, side),
        grid=(images,),
        in_specs=[
            pl.BlockSpec(memory_space=pltpu.SMEM),
            pl.BlockSpec((1, side, 2, 2 * side, c_prev), lambda i: (i, 0, 0, 0, 0)),
        ],
        out_specs=[
            pl.BlockSpec((4, per_image, c_prev), lambda i: (0, i, 0)),
            mask_block,
            mask_block,
            mask_block,
        ],
        out_shape=[shaped((4, pixels, c_prev), BF16), mask_shape, mask_shape, mask_shape],
        compiler_params=params(),
        cost_estimate=cost(0, 5 * pixels * c_prev),
        name="parity_images",
    )(tile_centres, x6)
    quarter, phases, mask_down, mask_back, mask_mid, cnt = lax.optimization_barrier(
        (quarter, phases, mask_down, mask_back, mask_mid, cnt)
    )
    piece = quarter[:, :tap_rows]
    down_rest = in_order(piece, send_to_groups(piece))
    early_piece = lax.optimization_barrier((quarter[:, tap_rows:], down_rest))[0]
    early_got = send_to_groups(early_piece)

    def scratch(channels):
        return [pltpu.VMEM((8, channels), F32), pltpu.VMEM((8, 128), F32)]

    z, st = [None] * layers, [None] * layers
    z[0], st[0] = pl.pallas_call(
        functools.partial(first_kernel, side),
        grid=(steps,),
        in_specs=[
            pl.BlockSpec((4, rows, c_prev), lambda i: (0, i, 0)),
            mask_spec,
            valid_spec,
            weights[0][1],
            single(down_rest.shape),
        ],
        out_specs=[tall(width), fixed((devices, 2, width))],
        out_shape=[shaped((pixels, width), F32), stat_shape(width)],
        scratch_shapes=scratch(width),
        compiler_params=params(),
        cost_estimate=cost(9 * pixels * c_prev * width, 6 * pixels * width),
        name="down_forward",
    )(phases, mask_down, valid, full_down, down_rest)

    *early_got, first_gathered = lax.optimization_barrier((*early_got, exchange(st[0])))
    early = in_order(early_piece, early_got)
    weights[1] = (early, single((2, *early.shape[1:]), (0, 0, 0, 0)))
    for k, layer in enumerate([2 + 2 * b for b in range(blocks)] + [layers - 2]):
        weights[layer] = (early, narrow_spec(k))

    inputs = [None] * layers
    moment = [None] * layers

    def forward(layer, kind, extra=(), extra_specs=(), gathered=None):
        prev, channels = layer - 1, widths[layer - 1]
        w, w_spec = weights[layer]
        if gathered is None:
            gathered = exchange(st[prev])
        args = [z[prev], gathered, cnt, gains[prev], biases[prev], valid, w, *extra]
        specs = [
            tall(channels),
            fixed((devices, 2, channels)),
            smem,
            fixed((1, channels)),
            fixed((1, channels)),
            valid_spec,
            w_spec,
            *extra_specs,
        ]
        v_width = 2 * half if kind == "join" else channels
        out_specs, out_shape = [tall(v_width)], [shaped((pixels, v_width), BF16)]
        if kind in ("split", "resid"):
            out_specs.append(tall(half))
            out_shape.append(shaped((pixels, half), F32))
        n = widths[layer]
        out_specs += [fixed((8, channels)), tall(n), fixed((devices, 2, n))]
        out_shape += [shaped((8, channels), F32), shaped((pixels, n), F32), stat_shape(n)]
        outs = list(
            pl.pallas_call(
                functools.partial(forward_kernel, kind, side),
                grid=(steps,),
                in_specs=specs,
                out_specs=out_specs,
                out_shape=out_shape,
                scratch_shapes=scratch(n),
                compiler_params=params(),
                cost_estimate=cost(9 * pixels * half * half * int(kind == "three"), 8 * pixels * half + 4 * pixels * channels),
                name="forward_" + kind,
            )(*args)
        )
        inputs[layer] = outs.pop(0)
        keep = outs.pop(0) if kind in ("split", "resid") else None
        moment[prev], z[layer], st[layer] = outs
        return keep

    forward(1, "plain", gathered=first_gathered)
    stream = None
    for b in range(blocks):
        if b == 0:
            stream = forward(2, "split")
        else:
            stream = forward(2 + 2 * b, "resid", (stream,), (tall(half),))
        forward(3 + 2 * b, "three", (mask_mid,), (mask_spec,))
    forward(layers - 2, "resid", (stream,), (tall(half),))
    split_low = inputs[2]
    forward(layers - 1, "join", (split_low,), (tall(half),))

    last = layers - 1
    n = widths[last]
    output, moment[last], g, st_back = pl.pallas_call(
        top_kernel,
        grid=(steps,),
        in_specs=[
            tall(n),
            fixed((devices, 2, n)),
            smem,
            fixed((1, n)),
            fixed((1, n)),
            tall(n),
        ],
        out_specs=[tall(n), fixed((8, n)), tall(n), fixed((devices, 2, n))],
        out_shape=[
            shaped((pixels, n), BF16),
            shaped((8, n), F32),
            shaped((pixels, n), BF16),
            stat_shape(n),
        ],
        scratch_shapes=[pltpu.VMEM((8, n), F32)],
        compiler_params=params(),
        cost_estimate=cost(0, 8 * pixels * n),
        name="top",
    )(z[last], exchange(st[last]), cnt, gains[last], biases[last], cotangent.reshape(pixels, n))

    totals = [None] * layers
    dz = [None] * layers

    def backward(layer, kind, g, gathered, extra=(), extra_specs=()):
        prev, channels = layer - 1, widths[layer]
        cp = widths[prev]
        w, w_spec = weights[layer]
        depth = 2 * half if kind == "part" else (half if kind == "merge" else cp)
        args = [g, z[layer], moment[layer], gathered, gains[layer], valid, cnt, w]
        args += [z[prev], moment[prev], gains[prev], biases[prev], *extra]
        specs = [
            tall(channels),
            tall(channels),
            fixed((8, channels)),
            fixed((devices, 2, channels)),
            fixed((1, channels)),
            valid_spec,
            smem,
            w_spec,
            tall(cp),
            fixed((8, cp)),
            fixed((1, cp)),
            fixed((1, cp)),
            *extra_specs,
        ]
        out_specs = [tall(channels), fixed((8, channels))]
        out_shape = [shaped((pixels, channels), BF16), shaped((8, channels), F32)]
        if kind in ("part", "keep", "add"):
            out_specs.append(tall(half))
            out_shape.append(shaped((pixels, half), F32))
        out_specs += [tall(cp), fixed((devices, 2, cp))]
        out_shape += [shaped((pixels, cp), BF16), stat_shape(cp)]
        outs = list(
            pl.pallas_call(
                functools.partial(backward_kernel, kind, side, depth),
                grid=(steps,),
                in_specs=specs,
                out_specs=out_specs,
                out_shape=out_shape,
                scratch_shapes=[pltpu.VMEM((8, cp), F32)],
                compiler_params=params(),
                cost_estimate=cost(9 * pixels * half * half * int(kind == "three"), 8 * pixels * half + 4 * pixels * cp),
                name="backward_" + kind,
            )(*args)
        )
        dz[layer], totals[layer] = outs.pop(0), outs.pop(0)
        keep = outs.pop(0) if kind in ("part", "keep", "add") else None
        return outs[0], outs[1], keep

    def tap_grad(stride, x, lane_mask, dz_low, w_shape, first=0):
        return pl.pallas_call(
            functools.partial(weight_grad_kernel, stride, side, first),
            out_shape=shaped(w_shape, BF16),
            compiler_params=params(),
            cost_estimate=cost(9 * pixels * half * dz_low.shape[1], 2 * pixels * dz_low.shape[1]),
            name="weight_grad_" + str(stride),
        )(x, lane_mask, dz_low)

    def flat_grad(x, dz_low):
        return jnp.einsum("pk,pn->kn", x, dz_low, preferred_element_type=F32).astype(BF16)

    def scatter(grad):
        return lax.psum_scatter(grad, "fsdp", scatter_dimension=0, tiled=True)

    def sum_own_part(own):
        parts = own.reshape(groups, own.shape[0] // groups, own.shape[1])
        parts = lax.all_to_all(parts, "dp", 0, 0, tiled=True)
        return jnp.sum(parts.astype(F32), axis=0).astype(BF16)

    def give_back(part):
        sent = jnp.broadcast_to(part[None], (groups, *part.shape))
        return lax.all_to_all(sent, "dp", 0, 0, tiled=True).astype(F32)

    def beside(st_back, grad, *due):
        return lax.optimization_barrier((exchange(st_back), grad, *due))[:2]

    g, st_back, grad_route = backward(last, "part", g, exchange(st_back))
    grad_unite = flat_grad(inputs[last], dz[last])
    gathered, grad_unite = beside(st_back, grad_unite)
    own_unite = scatter(grad_unite)
    g, st_back, grad_stream = backward(last - 1, "keep", g, gathered)
    narrow_grads = [None] * (blocks + 1)
    narrow_grads[blocks] = flat_grad(inputs[last - 1], dz[last - 1])
    gathered, narrow_grads[blocks] = beside(st_back, narrow_grads[blocks])
    own_spread = [None] * blocks
    for b in reversed(range(blocks)):
        layer = 3 + 2 * b
        g, st_back, _ = backward(layer, "three", g, gathered, (mask_mid,), (mask_spec,))
        own = tap_grad(1, inputs[layer], mask_mid, dz[layer], full_spread[b].shape)
        due = (own_unite,) if b == blocks - 1 else ()
        gathered, own = beside(st_back, own, *due)
        own_spread[b] = scatter(own)
        layer = 2 + 2 * b
        if b > 0:
            g, st_back, grad_stream = backward(
                layer, "add", g, gathered, (grad_stream,), (tall(half),)
            )
            low = inputs[layer]
        else:
            g, st_back, _ = backward(
                layer, "merge", g, gathered, (grad_stream, grad_route), (tall(half), tall(half))
            )
            low = inputs[layer][:, half:]
        narrow_grads[b] = flat_grad(low, dz[layer])
        due = own_spread[1:2] if b == 0 else ()
        gathered, narrow_grads[b] = beside(st_back, narrow_grads[b], *due)
    g, st_back, _ = backward(1, "plain", g, gathered)
    split_grads = [flat_grad(inputs[1], dz[1][:, k : k + half]) for k in range(0, width, half)]
    late = [w.reshape(fsdp, -1, half) for w in (*split_grads, *narrow_grads)]
    gathered, grad_late = beside(st_back, jnp.concatenate(late, axis=1))
    own_late = scatter(grad_late)[0]
    dz[0], totals[0] = pl.pallas_call(
        last_norm_kernel,
        grid=(steps,),
        in_specs=[
            tall(width),
            tall(width),
            fixed((8, width)),
            fixed((devices, 2, width)),
            fixed((1, width)),
            valid_spec,
            smem,
        ],
        out_specs=[tall(width), fixed((8, width))],
        out_shape=[shaped((pixels, width), BF16), shaped((8, width), F32)],
        compiler_params=params(),
        cost_estimate=cost(0, 5 * pixels * width),
        name="down_norm",
    )(g, z[0], moment[0], gathered, gains[0], valid, cnt)
    direct = tap_grad(2, phases, mask_down, dz[0], full_down.shape)
    own_direct = scatter(direct)
    dz_low = lax.optimization_barrier((dz[0], direct, own_spread[0]))[0]
    rest = tap_grad(2, phases, mask_down, dz_low, (groups, c_prev, width), taps)
    first_packed = lax.optimization_barrier((*own_spread, own_unite, direct))[:-1]
    first_packed = [o.reshape(-1, half) for o in first_packed]
    first_part = sum_own_part(jnp.concatenate(first_packed, axis=0))
    first_part, rest = lax.optimization_barrier((first_part, rest))
    rest_held, rest_got = deal(rest)
    *rest_held, dz_low = lax.optimization_barrier((*rest_held, dz_low))
    input_grad = pl.pallas_call(
        functools.partial(input_grad_kernel, side),
        grid=(images,),
        in_specs=[
            pl.BlockSpec((per_image, width), lambda i: (i, 0)),
            pl.BlockSpec((9, per_image, 128), lambda i: (0, i, 0)),
            weights[0][1],
            single(down_rest.shape),
        ],
        out_specs=pl.BlockSpec((1, side, 2, 2 * side, c_prev), lambda i: (i, 0, 0, 0, 0)),
        out_shape=shaped(x6.shape, BF16),
        compiler_params=params(),
        cost_estimate=cost(9 * pixels * c_prev * width, 8 * pixels * width),
        name="input_grad",
    )(dz_low, mask_back, full_down, down_rest).reshape(segment_input.shape)

    *received, input_grad = lax.optimization_barrier((*rest_got, input_grad))
    rest_sum = add_parts(rest_held[0], received)
    own_rest = scatter(rest_sum)
    *totals, rest_sum = lax.optimization_barrier((*totals, rest_sum))
    *moment, rest_sum = lax.optimization_barrier((*moment, rest_sum))
    first_part = lax.optimization_barrier((first_part, rest_sum))[0]
    first_sums = give_back(first_part).reshape(-1, half)
    own_late, own_direct, first_sums = lax.optimization_barrier((own_late, own_direct, first_sums))
    second = [own_late, own_direct.reshape(-1, width)]
    cut = [o.reshape(groups, -1, o.shape[-1]) for o in second]
    cut[1] = cut[1].reshape(groups, -1, half)
    second_part = sum_own_part(jnp.concatenate(cut, axis=1).reshape(-1, half))
    late_rows = own_late.shape[0]
    late_own = late_rows // groups
    sums = give_back(second_part)
    grad_direct = sums[:, late_own:].reshape(own_direct.shape[1:])
    late_sums = sums[:, :late_own].reshape(-1, half)
    spread_rows = first_packed[0].shape[0]
    split_parts = late_sums[:split_rows].reshape(-1, split_rows // 2, half)
    grad_split = jnp.concatenate([split_parts[0], split_parts[1]], axis=1)
    narrow = late_sums[split_rows:].reshape(blocks + 1, narrow_rows, 1, half)
    grad_spread = first_sums[: blocks * spread_rows]
    grad_spread = grad_spread.reshape(blocks, 9, narrow_rows, half).transpose(0, 2, 1, 3)
    grad_unite = first_sums[blocks * spread_rows :].reshape(own_unite.shape)[:, None]
    grad_split, narrow, grad_spread, grad_unite, grad_direct, own_rest = lax.optimization_barrier(
        (grad_split, narrow, grad_spread, grad_unite, grad_direct, own_rest)
    )
    grad_down = jnp.concatenate([grad_direct, give_back(own_rest)], axis=0).transpose(1, 0, 2)

    means = jnp.concatenate([m[0] for m in moment])
    variances = jnp.concatenate([m[1] for m in moment])
    new_mean = (1.0 - momentum_rate) * running_mean + momentum_rate * means
    new_var = (1.0 - momentum_rate) * running_var + momentum_rate * variances * whole_count / (
        whole_count - 1.0
    )
    return (
        output.reshape(cotangent.shape),
        input_grad,
        grad_down,
        grad_split[:, None],
        narrow[:blocks],
        grad_spread,
        narrow[blocks],
        grad_unite,
        jnp.concatenate([t[1] for t in totals]),
        jnp.concatenate([t[0] for t in totals]),
        new_mean,
        new_var,
    )


def solution(mesh):
    image = P(ALL, None, None, None)
    row3 = P("fsdp", None, None)
    row4 = P(None, "fsdp", None, None)
    return jax.shard_map(
        per_device,
        mesh=mesh,
        in_specs=(
            image,
            image,
            P(ALL, None),
            P(ALL, None, None),
            row3,
            row3,
            row4,
            row4,
            row3,
            row3,
            P(),
            P(),
            P(),
            P(),
        ),
        out_specs=(image, image, row3, row3, row4, row4, row3, row3, P(), P(), P(), P()),
        check_vma=False,
    )
```

```python
import functools

import jax
import jax.numpy as jnp
from jax import lax
from jax.experimental import pallas as pl
from jax.experimental.pallas import tpu as pltpu
from jax.sharding import PartitionSpec as P

norm_eps = 1e-05
momentum_rate = 0.1
ALL = ("dp", "fsdp")
F32 = jnp.float32
BF16 = jnp.bfloat16
VMEM_LIMIT = 58 * 1024 * 1024


def params():
    return pltpu.CompilerParams(vmem_limit_bytes=VMEM_LIMIT)


def cost(products, elements):
    return pl.CostEstimate(flops=2 * products, transcendentals=0, bytes_accessed=4 * elements)


def mish_parts(y):
    e = jnp.exp(jnp.minimum(y, 20.0))
    n = e * (e + 2.0)
    return e, n, 1.0 / (n + 2.0)


def mish(y):
    _, n, r = mish_parts(y)
    return y * (n * r)


def mish_slope(y):
    e, n, r = mish_parts(y)
    return r * (n + (4.0 * y) * ((n - e) * r))


def mish_both(y):
    e, n, r = mish_parts(y)
    return y * (n * r), r * (n + (4.0 * y) * ((n - e) * r))


def col_shift(x, step):
    if step == 0:
        return x
    rows = x.shape[0]
    return pltpu.roll(x.astype(F32), (-step) % rows, 0).astype(BF16)


def row_shift(x, step):
    if step == 0:
        return x
    if step > 0:
        return jnp.concatenate([x[step:], x[:step]], axis=0)
    return jnp.concatenate([x[step:], x[: x.shape[0] + step]], axis=0)


def masked(x, lane_mask):
    reps = x.shape[1] // 128
    return x * jnp.concatenate([lane_mask] * reps, axis=1)


def tap_weight(w_ref, tap):
    w = w_ref[:, tap]
    return w.reshape(w.shape[0] * w.shape[1], w.shape[2])


def down_weight(direct_ref, spread_ref, tap):
    taps = direct_ref.shape[1]
    if tap < taps:
        return tap_weight(direct_ref, tap)
    w = spread_ref[tap - taps]
    shards, held, half = w.shape
    own = held // 2
    sides = [w[:, k : k + own].reshape(shards * own, half) for k in (0, own)]
    return jnp.concatenate(sides, axis=1)


def column_blocks(w_ref, depth):
    if len(w_ref.shape) == 2:
        return [w_ref[...]]
    return [w_ref[k].reshape(depth, w_ref.shape[3]) for k in range(w_ref.shape[0])]


def dot_nn(a, b):
    return lax.dot_general(a, b, (((1,), (0,)), ((), ())), preferred_element_type=F32)


def dot_nt(a, b):
    return lax.dot_general(a, b, (((1,), (1,)), ((), ())), preferred_element_type=F32)


def dot_tn(a, b):
    return lax.dot_general(a, b, (((0,), (0,)), ((), ())), preferred_element_type=F32)


def mid_taps(x, side):
    cols = [col_shift(x, b - 1) for b in range(3)]
    for tap in range(9):
        a, b = divmod(tap, 3)
        yield tap, row_shift(cols[b], side * (a - 1))


def down_taps(phase, side):
    cols = {}
    for pr in range(2):
        for b in range(3):
            x = phase(2 * pr + int(b != 1))
            cols[pr, b] = col_shift(x, -1) if b == 0 else x
    for tap in range(9):
        a, b = divmod(tap, 3)
        yield tap, row_shift(cols[int(a != 1), b], -side if a == 0 else 0)


def device_total(s_ref):
    count, _, channels = s_ref.shape
    start = jnp.zeros((2, channels), F32)
    return lax.fori_loop(0, count, lambda i, t: t + s_ref[i], start, unroll=8)


def moments(s_ref, cnt_ref):
    count = s_ref.shape[0]
    total = device_total(s_ref)
    inv_n = cnt_ref[2 * count + 1]
    mean = total[0:1] * inv_n

    def spread(i, t):
        d = s_ref[i][0:1] - cnt_ref[i] * mean
        return t + d * d * cnt_ref[count + i]

    between = lax.fori_loop(0, count, spread, jnp.zeros_like(mean), unroll=8)
    var = (total[1:2] + between) * inv_n
    return mean, var, lax.rsqrt(var + norm_eps)


def kept_moments(s_ref, cnt_ref, mv_ref):
    @pl.when(pl.program_id(0) == 0)
    def _():
        mean, var, inv = moments(s_ref, cnt_ref)
        mv_ref[0:1] = mean
        mv_ref[1:2] = var
        mv_ref[2:3] = inv
        mv_ref[3:8] = jnp.zeros((5, mean.shape[1]), F32)

    return mv_ref[0:1], mv_ref[2:3]


def collect_moments(out, valid, acc_ref, num_ref, st_ref):
    step = pl.program_id(0)
    n = jnp.sum(valid, axis=0, keepdims=True)
    total = jnp.sum(out * valid, axis=0, keepdims=True)
    mean = total / jnp.maximum(n, 1.0)
    centred = out - mean
    squares = jnp.sum(valid * centred * centred, axis=0, keepdims=True)

    @pl.when(step == 0)
    def _():
        acc_ref[0:1] = total
        acc_ref[1:2] = squares
        num_ref[0:1] = jnp.broadcast_to(n, (1, 128))

    @pl.when(step > 0)
    def _():
        n_old = num_ref[0:1, 0:1]
        n_new = n_old + n
        old_mean = acc_ref[0:1] / jnp.maximum(n_old, 1.0)
        gap = mean - old_mean
        acc_ref[0:1] = acc_ref[0:1] + total
        acc_ref[1:2] = acc_ref[1:2] + squares + gap * gap * (n * n_old / jnp.maximum(n_new, 1.0))
        num_ref[0:1] = jnp.broadcast_to(n_new, (1, 128))

    @pl.when(step == pl.num_programs(0) - 1)
    def _():
        st_ref[...] = jnp.broadcast_to(acc_ref[0:2][None], st_ref.shape)


def collect_sums(g, xhat, acc_ref, st_ref):
    step = pl.program_id(0)
    first = jnp.sum(g, axis=0, keepdims=True)
    second = jnp.sum(g * xhat, axis=0, keepdims=True)

    @pl.when(step == 0)
    def _():
        acc_ref[0:1] = first
        acc_ref[1:2] = second

    @pl.when(step > 0)
    def _():
        acc_ref[0:1] = acc_ref[0:1] + first
        acc_ref[1:2] = acc_ref[1:2] + second

    @pl.when(step == pl.num_programs(0) - 1)
    def _():
        st_ref[...] = jnp.broadcast_to(acc_ref[0:2][None], st_ref.shape)


def prep_kernel(side, centre_ref, x_ref, ph_ref, down_ref, back_ref, mid_ref):
    half = ph_ref.shape[1]
    p = lax.broadcasted_iota(jnp.int32, (half, 2 * half), 0)
    s = lax.broadcasted_iota(jnp.int32, (half, 2 * half), 1)
    for pr in range(2):
        x = x_ref[0, :, pr]
        x = x.reshape(2 * half, x.shape[-1])
        for pc in range(2):
            pick = jnp.where(s == 2 * p + pc, 1.0, 0.0).astype(BF16)
            ph_ref[2 * pr + pc] = dot_nn(pick, x).astype(BF16)

    image = pl.program_id(0)
    pixel = lax.broadcasted_iota(jnp.int32, (half, 128), 0)
    spots = (pixel // side, pixel % side)
    centre = (centre_ref[image, 0], centre_ref[image, 1])

    def inside(own, other, middle, extent):
        same = (other >= middle) == (own >= middle)
        return jnp.where(same & (other >= 0) & (other < extent), 1.0, 0.0)

    down, back, mid = [], [], []
    for axis in range(2):
        at, middle = spots[axis], centre[axis]
        down.append([inside(2 * at, 2 * at + a - 1, middle, 2 * side) for a in range(3)])
        mid.append([inside(2 * at, 2 * (at + a - 1), middle, 2 * side) for a in range(3)])
        moved = []
        for a in range(3):
            to = at + int(a == 0)
            hit = inside(2 * to, 2 * to + a - 1, middle, 2 * side)
            moved.append(jnp.where(to < side, hit, 0.0))
        back.append(moved)
    for ref, parts in ((down_ref, down), (back_ref, back), (mid_ref, mid)):
        for tap in range(9):
            a, b = divmod(tap, 3)
            ref[tap] = (parts[0][a] * parts[1][b]).astype(BF16)


def first_kernel(
    side, ph_ref, m_ref, valid_ref, wa_ref, wb_ref, z_ref, st_ref, acc_ref, num_ref
):
    out = None
    for tap, x in down_taps(lambda k: ph_ref[k], side):
        part = dot_nn(masked(x, m_ref[tap]), down_weight(wa_ref, wb_ref, tap))
        out = part if out is None else out + part
    z_ref[...] = out
    collect_moments(out, valid_ref[...], acc_ref, num_ref, st_ref)


def forward_kernel(kind, side, z_ref, s_ref, cnt_ref, gain_ref, bias_ref, valid_ref, w_ref, *rest):
    rest = list(rest)
    m_ref = rest.pop(0) if kind == "three" else None
    other_ref = rest.pop(0) if kind in ("resid", "join") else None
    v_ref = rest.pop(0)
    keep_ref = rest.pop(0) if kind in ("split", "resid") else None
    mv_ref, out_ref, st_ref, acc_ref, num_ref = rest
    mean, inv = kept_moments(s_ref, cnt_ref, mv_ref)
    act = mish(((z_ref[...] - mean) * inv) * gain_ref[...] + bias_ref[...])
    if kind == "split":
        half = act.shape[1] // 2
        low = act.astype(BF16)
        v_ref[...] = low
        keep_ref[...] = act[:, half:]
        v = low[:, half:]
    elif kind == "resid":
        act = other_ref[...] + act
        keep_ref[...] = act
        v = act.astype(BF16)
        v_ref[...] = v
    elif kind == "join":
        v = jnp.concatenate([other_ref[...], act.astype(BF16)], axis=1)
        v_ref[...] = v
    else:
        v = act.astype(BF16)
        v_ref[...] = v
    if kind == "three":
        out = None
        for tap, x in mid_taps(v, side):
            part = dot_nn(masked(x, m_ref[tap]), tap_weight(w_ref, tap))
            out = part if out is None else out + part
    else:
        outs = [dot_nn(v, w) for w in column_blocks(w_ref, v.shape[1])]
        out = outs[0] if len(outs) == 1 else jnp.concatenate(outs, axis=1)
    out_ref[...] = out
    collect_moments(out, valid_ref[...], acc_ref, num_ref, st_ref)


def top_kernel(
    z_ref, s_ref, cnt_ref, gain_ref, bias_ref, cot_ref, o_ref, mv_ref, g_ref, st_ref, acc_ref
):
    mean, inv = kept_moments(s_ref, cnt_ref, mv_ref)
    xhat = (z_ref[...] - mean) * inv
    act, slope = mish_both(xhat * gain_ref[...] + bias_ref[...])
    o_ref[...] = act.astype(BF16)
    g = cot_ref[...].astype(F32) * slope
    g_ref[...] = g.astype(BF16)
    collect_sums(g, xhat, acc_ref, st_ref)


def norm_grad(g_ref, z_ref, mv_ref, s_ref, gain_ref, valid_ref, cnt_ref, tot_ref):
    @pl.when(pl.program_id(0) == 0)
    def _():
        total = device_total(s_ref)
        tot_ref[0:2] = total
        tot_ref[2:8] = jnp.zeros((6, total.shape[1]), F32)

    total = tot_ref[0:2]
    inv = mv_ref[2:3]
    inv_n = cnt_ref[2 * s_ref.shape[0] + 1]
    xhat = (z_ref[...] - mv_ref[0:1]) * inv
    mean_part = (valid_ref[...] * inv_n) * (total[0:1] + xhat * total[1:2])
    return (gain_ref[...] * inv * (g_ref[...].astype(F32) - mean_part)).astype(BF16)


def backward_kernel(
    kind,
    side,
    depth,
    g_ref,
    z_ref,
    mv_ref,
    s_ref,
    gain_ref,
    valid_ref,
    cnt_ref,
    w_ref,
    zp_ref,
    mvp_ref,
    gainp_ref,
    biasp_ref,
    *rest,
):
    rest = list(rest)
    m_ref = rest.pop(0) if kind == "three" else None
    add_ref = rest.pop(0) if kind in ("add", "merge") else None
    route_ref = rest.pop(0) if kind == "merge" else None
    dz_ref, tot_ref = rest.pop(0), rest.pop(0)
    keep_ref = rest.pop(0) if kind in ("part", "keep", "add") else None
    gp_ref, st_ref, acc_ref = rest
    dz = norm_grad(g_ref, z_ref, mv_ref, s_ref, gain_ref, valid_ref, cnt_ref, tot_ref)
    dz_ref[...] = dz
    if kind == "three":
        ga = None
        for tap, x in mid_taps(dz, side):
            part = dot_nt(masked(x, m_ref[tap]), tap_weight(w_ref, 8 - tap))
            ga = part if ga is None else ga + part
    else:
        ga, at = None, 0
        for w in column_blocks(w_ref, depth):
            part = dot_nt(dz[:, at : at + w.shape[1]], w)
            ga = part if ga is None else ga + part
            at += w.shape[1]
    if kind == "part":
        half = ga.shape[1] // 2
        keep_ref[...] = ga[:, :half]
        ga = ga[:, half:]
    elif kind == "keep":
        keep_ref[...] = ga
    elif kind == "add":
        ga = ga + add_ref[...]
        keep_ref[...] = ga
    elif kind == "merge":
        ga = jnp.concatenate([route_ref[...], ga + add_ref[...]], axis=1)
    xhat = (zp_ref[...] - mvp_ref[0:1]) * mvp_ref[2:3]
    gp = ga * mish_slope(xhat * gainp_ref[...] + biasp_ref[...])
    gp_ref[...] = gp.astype(BF16)
    collect_sums(gp, xhat, acc_ref, st_ref)


def last_norm_kernel(
    g_ref, z_ref, mv_ref, s_ref, gain_ref, valid_ref, cnt_ref, dz_ref, tot_ref
):
    dz_ref[...] = norm_grad(g_ref, z_ref, mv_ref, s_ref, gain_ref, valid_ref, cnt_ref, tot_ref)


def input_grad_kernel(side, dz_ref, m_ref, wa_ref, wb_ref, o_ref):
    dz = dz_ref[...]
    rows = dz.shape[0]
    moved = {}
    for dj in range(2):
        base = col_shift(dz, dj)
        for di in range(2):
            moved[di, dj] = row_shift(base, side * di)
    s = lax.broadcasted_iota(jnp.int32, (2 * rows, 2 * rows), 0)
    k = lax.broadcasted_iota(jnp.int32, (2 * rows, 2 * rows), 1)
    source = jnp.where(k < rows, 2 * k, 2 * (k - rows) + 1)
    put = jnp.where(s == source, 1.0, 0.0).astype(BF16)
    choices = (((1, 0),), ((2, 0), (0, 1)))
    for pr in range(2):
        both = []
        for pc in range(2):
            total = None
            for a, di in choices[pr]:
                for b, dj in choices[pc]:
                    tap = 3 * a + b
                    w = down_weight(wa_ref, wb_ref, tap)
                    part = dot_nt(masked(moved[di, dj], m_ref[tap]), w)
                    total = part if total is None else total + part
            both.append(total.astype(BF16))
        out = dot_nn(put, jnp.concatenate(both, axis=0)).astype(BF16)
        o_ref[0, :, pr] = out.reshape(side, 2 * side, out.shape[1])


def weight_grad_kernel(stride, side, first, x_ref, m_ref, dz_ref, o_ref):
    dz = dz_ref[...]
    by_shard = len(o_ref.shape) == 4
    count = o_ref.shape[1] if by_shard else o_ref.shape[0]
    taps = mid_taps(x_ref[...], side) if stride == 1 else down_taps(lambda k: x_ref[k], side)
    for tap, x in taps:
        if not first <= tap < first + count:
            continue
        grad = dot_tn(masked(x, m_ref[tap]), dz).astype(BF16)
        if by_shard:
            grad = grad.reshape(o_ref.shape[0], o_ref.shape[2], o_ref.shape[3])
            o_ref[:, tap - first] = grad
        else:
            o_ref[tap - first] = grad


def per_device(
    segment_input,
    cotangent,
    tile_centres,
    valid_mask,
    w_down,
    w_split,
    w_reduce,
    w_spread,
    w_trans,
    w_unite,
    bn_gain,
    bn_bias,
    running_mean,
    running_var,
):
    images, side, _, width = cotangent.shape
    half = w_trans.shape[2]
    c_prev = segment_input.shape[3]
    blocks = w_reduce.shape[0]
    per_image = side * side
    pixels = images * per_image
    fsdp = lax.axis_size("fsdp")
    devices = lax.axis_size("dp") * fsdp
    steps = images
    rows = pixels // steps

    def gather(shard):
        return lax.all_gather(shard, "fsdp", axis=0, tiled=False)

    groups = lax.axis_size("dp")
    taps = 9 - groups
    down = w_down.transpose(1, 0, 2)
    halves = [down[taps:, :, k : k + half] for k in range(0, width, half)]
    units = [w_split[:, 0, k : k + half] for k in range(0, width, half)]
    units += [w_reduce[b, :, 0] for b in range(blocks)] + [w_trans[:, 0]]
    units.append(jnp.zeros_like(w_trans[:, 0]))
    early = jnp.concatenate(units, axis=0).reshape(groups, -1, half)
    quarters = jnp.concatenate([*halves, early], axis=1)
    own_quarter = lax.dynamic_index_in_dim(quarters, lax.axis_index("dp"), 0, keepdims=False)
    quarter = gather(own_quarter)
    full_down = gather(lax.optimization_barrier((down[:taps], own_quarter))[0])
    tap_rows = 2 * down.shape[1]
    narrow_rows = w_trans.shape[0]
    split_rows = 2 * w_split.shape[0]

    group = lax.axis_index("dp")

    def to_group(x, k):
        return lax.ppermute(x, "dp", [(i, i ^ k) for i in range(groups)])

    def send_to_groups(piece):
        return [to_group(piece, k) for k in range(1, groups)]

    def in_order(piece, received):
        held = jnp.zeros((groups, *piece.shape), piece.dtype)
        for k, got in enumerate([piece, *received]):
            held = lax.dynamic_update_index_in_dim(held, got, group ^ k, 0)
        return held

    def deal(parts):
        held = [lax.dynamic_index_in_dim(parts, group ^ k, 0, False) for k in range(groups)]
        return held, [to_group(held[k], k) for k in range(1, groups)]

    def add_parts(own, received):
        total = own.astype(F32)
        for got in received:
            total = total + got.astype(F32)
        return total.astype(BF16)

    full_spread = [gather(w_spread[b].transpose(1, 0, 2)) for b in range(blocks)]
    full_unite = lax.all_gather(w_unite[:, 0], "fsdp", axis=0, tiled=True)

    valid = valid_mask.astype(F32).reshape(pixels, 1)
    own_count = jnp.broadcast_to(jnp.sum(valid), (devices, 1, 128))
    counts = lax.all_to_all(own_count, ALL, 0, 0, tiled=True)[:, 0, 0]
    whole_count = jnp.sum(counts)
    cnt = jnp.concatenate(
        [counts, 1.0 / jnp.maximum(counts, 1.0), jnp.stack([whole_count, 1.0 / whole_count])]
    )

    def exchange(st):
        return lax.all_to_all(st, ALL, 0, 0, tiled=True)

    smem = pl.BlockSpec(memory_space=pltpu.SMEM)

    def fixed(shape):
        return pl.BlockSpec(shape, lambda i: (0,) * len(shape))

    def single(shape, index=None):
        index = index or (0,) * len(shape)
        return pl.BlockSpec(shape, lambda i: index, pipeline_mode=pl.Buffered(1))

    def tall(channels, column=0):
        return pl.BlockSpec((rows, channels), lambda i: (i, column))

    mask_spec = pl.BlockSpec((9, rows, 128), lambda i: (0, i, 0))
    valid_spec = pl.BlockSpec((rows, 1), lambda i: (i, 0))

    def shaped(shape, dtype):
        return jax.ShapeDtypeStruct(shape, dtype)

    def stat_shape(channels):
        return shaped((devices, 2, channels), F32)

    widths = [width, width] + [half] * (2 * blocks) + [half, width]
    starts = [sum(widths[:i]) for i in range(len(widths))]
    gains = [bn_gain[s : s + c].reshape(1, c) for s, c in zip(starts, widths)]
    biases = [bn_bias[s : s + c].reshape(1, c) for s, c in zip(starts, widths)]
    layers = len(widths)

    def narrow_spec(k):
        return single((1, fsdp, narrow_rows, half), (2 + k // 2, 0, k % 2, 0))

    weights = [None] * layers
    weights[0] = (full_down, single(full_down.shape))
    for b in range(blocks):
        weights[3 + 2 * b] = (full_spread[b], single(full_spread[b].shape))
    weights[layers - 1] = (full_unite, single(full_unite.shape))

    x6 = segment_input.reshape(images, side, 2, 2 * side, c_prev)
    mask_shape = shaped((9, pixels, 128), BF16)
    mask_block = pl.BlockSpec((9, per_image, 128), lambda i: (0, i, 0))
    phases, mask_down, mask_back, mask_mid = pl.pallas_call(
        functools.partial(prep_kernel, side),
        grid=(images,),
        in_specs=[
            pl.BlockSpec(memory_space=pltpu.SMEM),
            pl.BlockSpec((1, side, 2, 2 * side, c_prev), lambda i: (i, 0, 0, 0, 0)),
        ],
        out_specs=[
            pl.BlockSpec((4, per_image, c_prev), lambda i: (0, i, 0)),
            mask_block,
            mask_block,
            mask_block,
        ],
        out_shape=[shaped((4, pixels, c_prev), BF16), mask_shape, mask_shape, mask_shape],
        compiler_params=params(),
        cost_estimate=cost(0, 5 * pixels * c_prev),
        name="parity_images",
    )(tile_centres, x6)
    quarter, phases, mask_down, mask_back, mask_mid, cnt = lax.optimization_barrier(
        (quarter, phases, mask_down, mask_back, mask_mid, cnt)
    )
    piece = quarter[:, :tap_rows]
    down_rest = in_order(piece, send_to_groups(piece))
    early_piece = lax.optimization_barrier((quarter[:, tap_rows:], down_rest))[0]
    early_got = send_to_groups(early_piece)

    def scratch(channels):
        return [pltpu.VMEM((8, channels), F32), pltpu.VMEM((8, 128), F32)]

    z, st = [None] * layers, [None] * layers
    z[0], st[0] = pl.pallas_call(
        functools.partial(first_kernel, side),
        grid=(steps,),
        in_specs=[
            pl.BlockSpec((4, rows, c_prev), lambda i: (0, i, 0)),
            mask_spec,
            valid_spec,
            weights[0][1],
            single(down_rest.shape),
        ],
        out_specs=[tall(width), fixed((devices, 2, width))],
        out_shape=[shaped((pixels, width), F32), stat_shape(width)],
        scratch_shapes=scratch(width),
        compiler_params=params(),
        cost_estimate=cost(9 * pixels * c_prev * width, 6 * pixels * width),
        name="down_forward",
    )(phases, mask_down, valid, full_down, down_rest)

    *early_got, first_gathered = lax.optimization_barrier((*early_got, exchange(st[0])))
    early = in_order(early_piece, early_got)
    weights[1] = (early, single((2, *early.shape[1:]), (0, 0, 0, 0)))
    for k, layer in enumerate([2 + 2 * b for b in range(blocks)] + [layers - 2]):
        weights[layer] = (early, narrow_spec(k))

    inputs = [None] * layers
    moment = [None] * layers

    def forward(layer, kind, extra=(), extra_specs=(), gathered=None):
        prev, channels = layer - 1, widths[layer - 1]
        w, w_spec = weights[layer]
        if gathered is None:
            gathered = exchange(st[prev])
        args = [z[prev], gathered, cnt, gains[prev], biases[prev], valid, w, *extra]
        specs = [
            tall(channels),
            fixed((devices, 2, channels)),
            smem,
            fixed((1, channels)),
            fixed((1, channels)),
            valid_spec,
            w_spec,
            *extra_specs,
        ]
        v_width = 2 * half if kind == "join" else channels
        out_specs, out_shape = [tall(v_width)], [shaped((pixels, v_width), BF16)]
        if kind in ("split", "resid"):
            out_specs.append(tall(half))
            out_shape.append(shaped((pixels, half), F32))
        n = widths[layer]
        out_specs += [fixed((8, channels)), tall(n), fixed((devices, 2, n))]
        out_shape += [shaped((8, channels), F32), shaped((pixels, n), F32), stat_shape(n)]
        outs = list(
            pl.pallas_call(
                functools.partial(forward_kernel, kind, side),
                grid=(steps,),
                in_specs=specs,
                out_specs=out_specs,
                out_shape=out_shape,
                scratch_shapes=scratch(n),
                compiler_params=params(),
                cost_estimate=cost(9 * pixels * half * half * int(kind == "three"), 8 * pixels * half + 4 * pixels * channels),
                name="forward_" + kind,
            )(*args)
        )
        inputs[layer] = outs.pop(0)
        keep = outs.pop(0) if kind in ("split", "resid") else None
        moment[prev], z[layer], st[layer] = outs
        return keep

    forward(1, "plain", gathered=first_gathered)
    stream = None
    for b in range(blocks):
        if b == 0:
            stream = forward(2, "split")
        else:
            stream = forward(2 + 2 * b, "resid", (stream,), (tall(half),))
        forward(3 + 2 * b, "three", (mask_mid,), (mask_spec,))
    forward(layers - 2, "resid", (stream,), (tall(half),))
    split_low = inputs[2]
    forward(layers - 1, "join", (split_low,), (tall(half),))

    last = layers - 1
    n = widths[last]
    output, moment[last], g, st_back = pl.pallas_call(
        top_kernel,
        grid=(steps,),
        in_specs=[
            tall(n),
            fixed((devices, 2, n)),
            smem,
            fixed((1, n)),
            fixed((1, n)),
            tall(n),
        ],
        out_specs=[tall(n), fixed((8, n)), tall(n), fixed((devices, 2, n))],
        out_shape=[
            shaped((pixels, n), BF16),
            shaped((8, n), F32),
            shaped((pixels, n), BF16),
            stat_shape(n),
        ],
        scratch_shapes=[pltpu.VMEM((8, n), F32)],
        compiler_params=params(),
        cost_estimate=cost(0, 8 * pixels * n),
        name="top",
    )(z[last], exchange(st[last]), cnt, gains[last], biases[last], cotangent.reshape(pixels, n))

    totals = [None] * layers
    dz = [None] * layers

    def backward(layer, kind, g, gathered, extra=(), extra_specs=()):
        prev, channels = layer - 1, widths[layer]
        cp = widths[prev]
        w, w_spec = weights[layer]
        depth = 2 * half if kind == "part" else (half if kind == "merge" else cp)
        args = [g, z[layer], moment[layer], gathered, gains[layer], valid, cnt, w]
        args += [z[prev], moment[prev], gains[prev], biases[prev], *extra]
        specs = [
            tall(channels),
            tall(channels),
            fixed((8, channels)),
            fixed((devices, 2, channels)),
            fixed((1, channels)),
            valid_spec,
            smem,
            w_spec,
            tall(cp),
            fixed((8, cp)),
            fixed((1, cp)),
            fixed((1, cp)),
            *extra_specs,
        ]
        out_specs = [tall(channels), fixed((8, channels))]
        out_shape = [shaped((pixels, channels), BF16), shaped((8, channels), F32)]
        if kind in ("part", "keep", "add"):
            out_specs.append(tall(half))
            out_shape.append(shaped((pixels, half), F32))
        out_specs += [tall(cp), fixed((devices, 2, cp))]
        out_shape += [shaped((pixels, cp), BF16), stat_shape(cp)]
        outs = list(
            pl.pallas_call(
                functools.partial(backward_kernel, kind, side, depth),
                grid=(steps,),
                in_specs=specs,
                out_specs=out_specs,
                out_shape=out_shape,
                scratch_shapes=[pltpu.VMEM((8, cp), F32)],
                compiler_params=params(),
                cost_estimate=cost(9 * pixels * half * half * int(kind == "three"), 8 * pixels * half + 4 * pixels * cp),
                name="backward_" + kind,
            )(*args)
        )
        dz[layer], totals[layer] = outs.pop(0), outs.pop(0)
        keep = outs.pop(0) if kind in ("part", "keep", "add") else None
        return outs[0], outs[1], keep

    def tap_grad(stride, x, lane_mask, dz_low, w_shape, first=0):
        return pl.pallas_call(
            functools.partial(weight_grad_kernel, stride, side, first),
            out_shape=shaped(w_shape, BF16),
            compiler_params=params(),
            cost_estimate=cost(9 * pixels * half * dz_low.shape[1], 2 * pixels * dz_low.shape[1]),
            name="weight_grad_" + str(stride),
        )(x, lane_mask, dz_low)

    def flat_grad(x, dz_low):
        return jnp.einsum("pk,pn->kn", x, dz_low, preferred_element_type=F32).astype(BF16)

    def scatter(grad):
        return lax.psum_scatter(grad, "fsdp", scatter_dimension=0, tiled=True)

    def sum_own_part(own):
        parts = own.reshape(groups, own.shape[0] // groups, own.shape[1])
        parts = lax.all_to_all(parts, "dp", 0, 0, tiled=True)
        return jnp.sum(parts.astype(F32), axis=0).astype(BF16)

    def give_back(part):
        sent = jnp.broadcast_to(part[None], (groups, *part.shape))
        return lax.all_to_all(sent, "dp", 0, 0, tiled=True).astype(F32)

    def beside(st_back, grad, *due):
        return lax.optimization_barrier((exchange(st_back), grad, *due))[:2]

    g, st_back, grad_route = backward(last, "part", g, exchange(st_back))
    grad_unite = flat_grad(inputs[last], dz[last])
    gathered, grad_unite = beside(st_back, grad_unite)
    own_unite = scatter(grad_unite)
    g, st_back, grad_stream = backward(last - 1, "keep", g, gathered)
    narrow_grads = [None] * (blocks + 1)
    narrow_grads[blocks] = flat_grad(inputs[last - 1], dz[last - 1])
    gathered, narrow_grads[blocks] = beside(st_back, narrow_grads[blocks])
    own_spread = [None] * blocks
    for b in reversed(range(blocks)):
        layer = 3 + 2 * b
        g, st_back, _ = backward(layer, "three", g, gathered, (mask_mid,), (mask_spec,))
        if b > 0:
            own = tap_grad(1, inputs[layer], mask_mid, dz[layer], full_spread[b].shape)
            due = (own_unite,) if b == blocks - 1 else ()
            gathered, own = beside(st_back, own, *due)
        else:
            own_shape = (fsdp, taps, *full_spread[b].shape[2:])
            own = tap_grad(1, inputs[layer], mask_mid, dz[layer], own_shape)
            tail = tap_grad(1, inputs[layer], mask_mid, dz[layer], (groups, half, half), taps)
            gathered, own, tail = lax.optimization_barrier((exchange(st_back), own, tail))
            tail_held, tail_got = deal(tail)
        own_spread[b] = scatter(own)
        layer = 2 + 2 * b
        if b > 0:
            g, st_back, grad_stream = backward(
                layer, "add", g, gathered, (grad_stream,), (tall(half),)
            )
            low = inputs[layer]
        else:
            g, st_back, _ = backward(
                layer, "merge", g, gathered, (grad_stream, grad_route), (tall(half), tall(half))
            )
            low = inputs[layer][:, half:]
        narrow_grads[b] = flat_grad(low, dz[layer])
        due = own_spread[1:2] if b == 0 else ()
        gathered, narrow_grads[b] = beside(st_back, narrow_grads[b], *due)
    g, st_back, _ = backward(1, "plain", g, gathered)
    split_grads = [flat_grad(inputs[1], dz[1][:, k : k + half]) for k in range(0, width, half)]
    late = [w.reshape(fsdp, -1, half) for w in (*split_grads, *narrow_grads)]
    gathered, grad_late = beside(st_back, jnp.concatenate(late, axis=1), *tail_got)
    own_late = scatter(grad_late)[0]
    dz[0], totals[0] = pl.pallas_call(
        last_norm_kernel,
        grid=(steps,),
        in_specs=[
            tall(width),
            tall(width),
            fixed((8, width)),
            fixed((devices, 2, width)),
            fixed((1, width)),
            valid_spec,
            smem,
        ],
        out_specs=[tall(width), fixed((8, width))],
        out_shape=[shaped((pixels, width), BF16), shaped((8, width), F32)],
        compiler_params=params(),
        cost_estimate=cost(0, 5 * pixels * width),
        name="down_norm",
    )(g, z[0], moment[0], gathered, gains[0], valid, cnt)
    direct = tap_grad(2, phases, mask_down, dz[0], full_down.shape)
    own_direct = scatter(direct)
    dz_low = lax.optimization_barrier((dz[0], direct, own_spread[0]))[0]
    rest = tap_grad(2, phases, mask_down, dz_low, (groups, c_prev, width), taps)
    first_packed = lax.optimization_barrier((*own_spread, own_unite, direct))[:-1]
    first_packed = [o.reshape(-1, half) for o in first_packed]
    first_part = sum_own_part(jnp.concatenate(first_packed, axis=0))
    first_part, rest = lax.optimization_barrier((first_part, rest))
    rest_held, rest_got = deal(rest)
    *rest_held, dz_low = lax.optimization_barrier((*rest_held, dz_low))
    input_grad = pl.pallas_call(
        functools.partial(input_grad_kernel, side),
        grid=(images,),
        in_specs=[
            pl.BlockSpec((per_image, width), lambda i: (i, 0)),
            pl.BlockSpec((9, per_image, 128), lambda i: (0, i, 0)),
            weights[0][1],
            single(down_rest.shape),
        ],
        out_specs=pl.BlockSpec((1, side, 2, 2 * side, c_prev), lambda i: (i, 0, 0, 0, 0)),
        out_shape=shaped(x6.shape, BF16),
        compiler_params=params(),
        cost_estimate=cost(9 * pixels * c_prev * width, 8 * pixels * width),
        name="input_grad",
    )(dz_low, mask_back, full_down, down_rest).reshape(segment_input.shape)

    first_sums = give_back(first_part).reshape(-1, half)
    *received, input_grad, first_sums = lax.optimization_barrier(
        (*rest_got, input_grad, first_sums)
    )
    rest_sum = add_parts(rest_held[0], received)
    tail_sum = add_parts(tail_held[0], tail_got)
    summed = [rest_sum[:, k : k + half] for k in range(0, width, half)] + [tail_sum]
    summed = [part.reshape(fsdp, -1, half) for part in summed]
    own_summed = scatter(jnp.concatenate(summed, axis=1))[0]
    *totals, rest_sum = lax.optimization_barrier((*totals, rest_sum))
    *moment, rest_sum = lax.optimization_barrier((*moment, rest_sum))
    own_late, own_direct, first_sums = lax.optimization_barrier((own_late, own_direct, first_sums))
    second = [own_late, own_direct.reshape(-1, width)]
    cut = [o.reshape(groups, -1, o.shape[-1]) for o in second]
    cut[1] = cut[1].reshape(groups, -1, half)
    second_part = sum_own_part(jnp.concatenate(cut, axis=1).reshape(-1, half))
    late_rows = own_late.shape[0]
    late_own = late_rows // groups
    second_rows = second_part.shape[0]
    sums = give_back(jnp.concatenate([second_part, own_summed], axis=0))
    ends = sums[:, second_rows:]
    grad_direct = sums[:, late_own:second_rows].reshape(own_direct.shape[1:])
    late_sums = sums[:, :late_own].reshape(-1, half)
    split_parts = late_sums[:split_rows].reshape(-1, split_rows // 2, half)
    grad_split = jnp.concatenate([split_parts[0], split_parts[1]], axis=1)
    narrow = late_sums[split_rows:].reshape(blocks + 1, narrow_rows, 1, half)
    grad_rest = jnp.concatenate(
        [ends[:, k : k + tap_rows // 2] for k in range(0, tap_rows, tap_rows // 2)], axis=2
    )
    grad_down = jnp.concatenate([grad_direct, grad_rest], axis=0).transpose(1, 0, 2)
    at, spread = 0, []
    for b in range(blocks):
        size = first_packed[b].shape[0]
        spread.append(first_sums[at : at + size].reshape(-1, narrow_rows, half))
        at += size
    spread[0] = jnp.concatenate([spread[0], ends[:, tap_rows:]], axis=0)
    grad_spread = jnp.stack(spread).transpose(0, 2, 1, 3)
    grad_unite = first_sums[at:].reshape(own_unite.shape)[:, None]

    means = jnp.concatenate([m[0] for m in moment])
    variances = jnp.concatenate([m[1] for m in moment])
    new_mean = (1.0 - momentum_rate) * running_mean + momentum_rate * means
    new_var = (1.0 - momentum_rate) * running_var + momentum_rate * variances * whole_count / (
        whole_count - 1.0
    )
    return (
        output.reshape(cotangent.shape),
        input_grad,
        grad_down,
        grad_split[:, None],
        narrow[:blocks],
        grad_spread,
        narrow[blocks],
        grad_unite,
        jnp.concatenate([t[1] for t in totals]),
        jnp.concatenate([t[0] for t in totals]),
        new_mean,
        new_var,
    )


def solution(mesh):
    image = P(ALL, None, None, None)
    row3 = P("fsdp", None, None)
    row4 = P(None, "fsdp", None, None)
    return jax.shard_map(
        per_device,
        mesh=mesh,
        in_specs=(
            image,
            image,
            P(ALL, None),
            P(ALL, None, None),
            row3,
            row3,
            row4,
            row4,
            row3,
            row3,
            P(),
            P(),
            P(),
            P(),
        ),
        out_specs=(image, image, row3, row3, row4, row4, row3, row3, P(), P(), P(), P()),
        check_vma=False,
    )
```
